32 devices in a mesh: row: 2 (over core), col: 16 (over z, y, x).
Axes of the slice: x: 2, y: 2, z: 4, core: 2. Of those that a mesh axis runs over, the one named last changes fastest.
Arguments:
- mat_a: bfloat16 [5120, 24576], P('row', 'col'), may hold values from -6 to 6
- mat_b: bfloat16 [24576, 4096], P('row', 'col'), may hold values from -0.15625 to 0.15625
- mask_a: int32 [40, 192], P('row', 'col'), may hold values from 0 to 1, as said below
- mask_b: int32 [192, 32], P('row', 'col'), may hold values 0 or 1
Outputs:
- product: bfloat16 [5120, 4096], P('row', 'col')
The draws below stay inside these ranges and needn't reach their ends.
Inputs may be any that keep to these rules, and one draw needn't show every extreme that they name: `mask_a`: in each tile of 20 x 12 entries, the block rows holding an occupied block come first and each holds at least one; in every draw some tile has all 20 block rows occupied.
All inputs are finite; a program needn't handle non-finite values. No bound on the sum of `mask_b` on one device may be relied on, other than what follows from the above.
Results may differ from the reference program's by a relative error of at most 0.0025.
Values may be sent and summed in bfloat16 or wider, within the bound.
A program may use at most 128 MiB of HBM per device.

```python
import jax
import jax.numpy as jnp
from jax import lax

BLK = 128
RB = 20
KB = 12
CB = 2
SLOTS = 8
ROWS = 5120
INNER = 24576
COLS = 4096
N_ROW = 2
N_COL = 16


def draw_mask_a(key, part):
    keys = jax.random.split(jax.random.fold_in(key, 11), 5)
    heavy = jax.random.randint(keys[0], (N_ROW, N_COL), 0, 4) == 0
    light = jax.random.randint(keys[1], (N_ROW, N_COL), 1, min(4, RB) + 1)
    counts = jnp.where(heavy, RB, light)
    chosen = jax.random.randint(keys[2], (), 0, N_ROW * N_COL)
    places = jnp.arange(N_ROW * N_COL).reshape(N_ROW, N_COL)
    counts = jnp.where(places == chosen, RB, counts)
    blocks = jax.random.randint(keys[3], (N_ROW, RB, N_COL, KB), 0, 4) != 0
    needed = jax.random.randint(keys[4], (N_ROW, RB, N_COL, 1), 0, KB)
    blocks = jnp.logical_or(blocks, jnp.arange(KB)[None, None, None, :] == needed)
    living = jnp.arange(RB)[None, :, None, None] < counts[:, None, :, None]
    occupied = jnp.logical_and(blocks, living).astype(jnp.int32)
    return occupied.reshape(N_ROW * RB, N_COL * KB)


def touch_ends(drawn, own_key, smallest, high):
    longest = drawn.shape.index(max(drawn.shape))
    spots = []
    for shift in (0, 1):
        where = [jax.random.randint(jax.random.fold_in(own_key, axis), (), 0, length) for axis, length in enumerate(drawn.shape)]
        where[longest] = (where[longest] + shift) % drawn.shape[longest]
        spots.append(tuple(where))
    return drawn.at[spots[0]].set(smallest).at[spots[1]].set(high)


def steps_of(stream_key, shape, cuts, smallest, largest):
    def one(position, shards_of):
        heights = jax.random.uniform(jax.random.fold_in(jax.random.fold_in(stream_key, 6), position), (shards_of,), jnp.float32, smallest / len(cuts), largest / len(cuts))
        return jnp.repeat(jnp.exp(heights), shape[position] // shards_of).reshape((-1,) + (1,) * (len(shape) - position - 1))

    loudness = one(*cuts[0])
    for cut in cuts[1:]:
        loudness = loudness * one(*cut)
    return loudness


def gaussian(key, extent, scale, most, cuts=(), held_as=jnp.bfloat16):
    gain = steps_of(key, extent, cuts, -0.22, 0.18) if cuts else 1.0
    drawn = jax.random.normal(key, extent, jnp.float32) * scale * gain
    return jnp.minimum(jnp.maximum(drawn, -most), most).astype(held_as)


def setup_inputs(seed: int = 0) -> dict:
    splits = jax.random.split(jax.random.key(seed), 5)
    return {
        "mat_a": gaussian(splits[0], (ROWS, INNER), 1.0, 6.0, ((0, 2), (1, 16))),
        "mat_b": gaussian(splits[1], (INNER, COLS), (KB * BLK) ** -0.5, 0.15625, ((0, 2), (1, 16))),
        "mask_a": draw_mask_a(jax.random.fold_in(splits[4], 71), 0),
        "mask_b": touch_ends((jax.random.randint(splits[3], (N_COL * KB, N_COL * CB), 0, 4) < 3).astype(jnp.int32), jax.random.fold_in(splits[3], 1), 0, 1),
    }


def mask_blocks(matrix, occupied):
    rows, columns = occupied.shape
    blocked = matrix.reshape(rows, matrix.shape[0] // rows, columns, matrix.shape[1] // columns)
    scaling = occupied.astype(matrix.dtype)[:, None, :, None]
    return (blocked * scaling).reshape(matrix.shape)


def row_product(matrix_rows, right_tile, live_flags):
    stacked = matrix_rows.reshape(RB, BLK, matrix_rows.shape[1])

    def one_row(inputs):
        row_block, flagged = inputs
        return lax.cond(
            flagged,
            lambda piece: jnp.dot(piece, right_tile, preferred_element_type=jnp.float32),
            lambda piece: jnp.zeros((BLK, right_tile.shape[1]), jnp.float32),
            row_block,
        )

    return lax.map(one_row, (stacked, live_flags)).reshape(RB * BLK, right_tile.shape[1])


def reference(mat_a, mat_b, mask_a, mask_b):
    masked_a = mask_blocks(mat_a, mask_a)
    masked_b = mask_blocks(mat_b, mask_b)
    tiles_a = masked_a.reshape(N_ROW, RB * BLK, N_COL, KB * BLK).transpose(0, 2, 1, 3)
    stacked = masked_b.reshape(N_ROW, SLOTS, KB * BLK, N_COL, CB * BLK).transpose(0, 3, 1, 2, 4)
    first_b = stacked[:, :, 0]
    sent_b = jnp.concatenate([stacked[:1, :, 1], stacked[1:, :, 0]], axis=0)
    next_b = jnp.roll(sent_b, -1, axis=0)
    live_a = jnp.any(mask_a.reshape(N_ROW, RB, N_COL, KB) > 0, axis=3).transpose(0, 2, 1)
    next_a = jnp.roll(tiles_a, -1, axis=1)
    next_live = jnp.roll(live_a, -1, axis=1)
    count = N_ROW * N_COL
    inputs = (
        tiles_a.reshape(count, RB * BLK, KB * BLK),
        first_b.reshape(count, KB * BLK, CB * BLK),
        live_a.reshape(count, RB),
        next_a.reshape(count, RB * BLK, KB * BLK),
        next_b.reshape(count, KB * BLK, CB * BLK),
        next_live.reshape(count, RB),
    )

    def one_tile(pieces):
        first_a, first_right, first_live, second_a, second_right, second_live = pieces
        summed = row_product(first_a, first_right, first_live) + row_product(second_a, second_right, second_live)
        return summed.astype(jnp.bfloat16)

    result = lax.map(one_tile, inputs)
    result = result.reshape(N_ROW, N_COL, RB * BLK, CB * BLK).transpose(0, 2, 1, 3)
    return result.reshape(N_ROW * RB * BLK, N_COL * CB * BLK)
```

```python
import functools

import jax
import jax.numpy as jnp
from jax import lax
from jax.experimental import pallas as pl
from jax.experimental.pallas import tpu as pltpu
from jax.sharding import PartitionSpec as P

BLK = 128
LEVELS = 32767.0
TINY = 1e-33
MESH = pl.DeviceIdType.MESH


def times_flag(block, flag):
    scale = jnp.full(block.shape, flag.astype(jnp.float32)).astype(block.dtype)
    return block * scale


def kernel(
    group,
    a_hbm, b_hbm, flags_a, flags_b, out_hbm,
    a_tile, b_own, b_send, b_recv, own_sum, code_send, code_recv, step_send, step_recv, out_tile,
    a_sem, b_sem, o_sem, bs_sem, br_sem, cs_sem, cr_sem, ss_sem, sr_sem,
):
    n_row, n_col = lax.axis_size("row"), lax.axis_size("col")
    row, col = lax.axis_index("row"), lax.axis_index("col")
    up, down = lax.rem(row + n_row - 1, n_row), lax.rem(row + 1, n_row)
    left, right = lax.rem(col + n_col - 1, n_col), lax.rem(col + 1, n_col)
    rows, inner = a_tile.shape
    width = b_own.shape[1]
    deep, halves = inner // BLK, width // BLK
    span = group * BLK
    chunks = rows // span

    def piece(c):
        return pl.ds(pl.multiple_of(c * span, span), span)

    def load_a(c):
        return pltpu.make_async_copy(a_hbm.at[piece(c), :], a_tile.at[piece(c), :], a_sem.at[c])

    slot = jnp.where(row == 0, 1, 0)

    def load_send(h):
        return pltpu.make_async_copy(
            b_hbm.at[pl.ds(pl.multiple_of(slot * inner, inner), inner), h * BLK:(h + 1) * BLK], b_send.at[h], b_sem.at[h]
        )

    get_own = pltpu.make_async_copy(b_hbm.at[pl.ds(0, inner), :], b_own, b_sem.at[halves])

    barrier = pltpu.get_barrier_semaphore()
    pl.semaphore_signal(barrier, inc=1, device_id={"row": down, "col": left}, device_id_type=MESH)
    pl.semaphore_signal(barrier, inc=1, device_id={"row": down, "col": col}, device_id_type=MESH)
    for h in range(halves):
        load_send(h).start()
    get_own.start()
    for c in range(chunks):
        load_a(c).start()

    def move_b(h):
        return pltpu.make_async_remote_copy(
            src_ref=b_send.at[h], dst_ref=b_recv.at[h], send_sem=bs_sem.at[h], recv_sem=br_sem.at[h],
            device_id={"row": up, "col": right}, device_id_type=MESH,
        )

    for h in range(halves):
        load_send(h).wait()
        for k in range(deep):
            lines = slice(k * BLK, (k + 1) * BLK)
            b_send[h, lines, :] = times_flag(b_send[h, lines, :], flags_b[h, slot * deep + k])
        if h == 0:
            pl.semaphore_wait(barrier, 2)
        move_b(h).start()

    get_own.wait()
    for h in range(halves):
        for k in range(deep):
            spot = (slice(k * BLK, (k + 1) * BLK), slice(h * BLK, (h + 1) * BLK))
            b_own[spot] = times_flag(b_own[spot], flags_b[h, k])

    def own_part(c, carry):
        load_a(c).wait()
        for g in range(group):
            lines = pl.ds(pl.multiple_of(c * span + g * BLK, BLK), BLK)
            for k in range(deep):
                block = a_tile[lines, k * BLK:(k + 1) * BLK]
                a_tile[lines, k * BLK:(k + 1) * BLK] = times_flag(block, flags_a[k, c * group + g])
        own_sum[piece(c), :] = jnp.dot(a_tile[piece(c), :], b_own[...], preferred_element_type=jnp.float32)
        return carry

    lax.fori_loop(0, chunks, own_part, 0)

    def move_code(i):
        return pltpu.make_async_remote_copy(
            src_ref=code_send.at[i], dst_ref=code_recv.at[i], send_sem=cs_sem.at[i], recv_sem=cr_sem.at[i],
            device_id={"row": row, "col": left}, device_id_type=MESH,
        )

    def move_step(i):
        return pltpu.make_async_remote_copy(
            src_ref=step_send.at[i], dst_ref=step_recv.at[i], send_sem=ss_sem.at[i], recv_sem=sr_sem.at[i],
            device_id={"row": row, "col": left}, device_id_type=MESH,
        )

    def send_out(i, carry):
        move_step(i).start()
        move_code(i).start()
        return carry

    def next_part(h, early, c, carry):
        i = h * chunks + c
        value = jnp.dot(a_tile[piece(c), :], b_recv[h], preferred_element_type=jnp.float32)
        most = jnp.maximum(jnp.max(jnp.abs(value), axis=0, keepdims=True), TINY)
        step_send[i] = jnp.broadcast_to(most * (1.0 / LEVELS), step_send.shape[1:])
        code_send[i] = jnp.round(value * (LEVELS / most)).astype(jnp.int32).astype(jnp.int16)
        return carry if early else send_out(i, carry)

    for h in range(halves):
        move_b(h).wait_recv()
        if h == halves - 1:
            pass
        lax.fori_loop(0, chunks, functools.partial(next_part, h, h < halves - 1), 0)
        if h == halves - 2:
            for b in range(halves):
                move_b(b).wait_send()
            lax.fori_loop(0, (halves - 1) * chunks, send_out, 0)

    def put(i, h, c):
        return pltpu.make_async_copy(
            out_tile.at[piece(c), h * BLK:(h + 1) * BLK], out_hbm.at[piece(c), h * BLK:(h + 1) * BLK], o_sem.at[i]
        )

    for h in range(halves):

        def finish(c, carry, h=h):
            i = h * chunks + c
            move_step(i).wait_recv()
            move_code(i).wait_recv()
            code = code_recv[i].astype(jnp.int32).astype(jnp.float32)
            total = own_sum[piece(c), h * BLK:(h + 1) * BLK] + code * step_recv[i, 0:1, :]
            out_tile[piece(c), h * BLK:(h + 1) * BLK] = total.astype(out_tile.dtype)
            put(i, h, c).start()
            return carry

        lax.fori_loop(0, chunks, finish, 0)

    pass

    def sent(i, carry):
        move_step(i).wait_send()
        move_code(i).wait_send()
        return carry

    lax.fori_loop(0, halves * chunks, sent, 0)
    for h in range(halves):
        for c in range(chunks):
            put(h * chunks + c, h, c).wait()


def hand_on(pieces, source, target, held, in_sem, out_sem):
    span = source.shape[0] // pieces

    def fetch(n):
        return pltpu.make_async_copy(source.at[n * span:(n + 1) * span, :], held.at[n], in_sem.at[n])

    def put(n):
        return pltpu.make_async_copy(held.at[n], target.at[n * span:(n + 1) * span, :], out_sem.at[n])

    for n in range(pieces):
        fetch(n).start()
    for n in range(pieces):
        fetch(n).wait()
        put(n).start()
    for n in range(pieces):
        put(n).wait()


def pass_on(source, target, sem):
    copy = pltpu.make_async_copy(source, target, sem)
    copy.start()
    copy.wait()


def body(mat_a, mat_b, mask_a, mask_b):
    rows, inner = mat_a.shape
    width = mat_b.shape[1]
    block_rows = mask_a.shape[0]
    group = next(g for g in (4, 2, 1) if block_rows % g == 0)
    span = group * BLK
    chunks = rows // span
    halves = width // BLK
    sends = halves * chunks
    dma = pltpu.SemaphoreType.DMA
    product = pl.pallas_call(
        functools.partial(kernel, group),
        out_shape=jax.ShapeDtypeStruct((rows, width), jnp.bfloat16),
        in_specs=[
            pl.BlockSpec(memory_space=pl.ANY),
            pl.BlockSpec(memory_space=pl.ANY),
            pl.BlockSpec(memory_space=pltpu.SMEM),
            pl.BlockSpec(memory_space=pltpu.SMEM),
        ],
        out_specs=pl.BlockSpec(memory_space=pl.ANY),
        scratch_shapes=[
            pltpu.VMEM((rows, inner), jnp.bfloat16),
            pltpu.VMEM((inner, width), jnp.bfloat16),
            pltpu.VMEM((halves, inner, BLK), jnp.bfloat16),
            pltpu.VMEM((halves, inner, BLK), jnp.bfloat16),
            pltpu.VMEM((rows, width), jnp.float32),
            pltpu.VMEM((sends, span, BLK), jnp.int16),
            pltpu.VMEM((sends, span, BLK), jnp.int16),
            pltpu.VMEM((sends, 8, BLK), jnp.float32),
            pltpu.VMEM((sends, 8, BLK), jnp.float32),
            pltpu.VMEM((rows, width), jnp.bfloat16),
            dma((chunks,)), dma((halves + 1,)), dma((sends,)), dma((halves,)), dma((halves,)),
            dma((sends,)), dma((sends,)), dma((sends,)), dma((sends,)),
        ],
        compiler_params=pltpu.CompilerParams(collective_id=0, has_side_effects=True),
        name="cannon",
    )(mat_a, mat_b, mask_a.T, mask_b.T)
    pieces = chunks
    return pl.pallas_call(
        functools.partial(hand_on, pieces),
        out_shape=jax.ShapeDtypeStruct(product.shape, product.dtype),
        in_specs=[pl.BlockSpec(memory_space=pl.ANY)],
        out_specs=pl.BlockSpec(memory_space=pl.ANY),
        scratch_shapes=[
            pltpu.VMEM((pieces, rows // pieces, width), product.dtype),
            dma((pieces,)), dma((pieces,)),
        ],
        name="hand_on",
    )(product)


def solution(mesh):
    return jax.shard_map(
        body,
        mesh=mesh,
        in_specs=(P("row", "col"), P("row", "col"), P("row", "col"), P("row", "col")),
        out_specs=P("row", "col"),
        check_vma=False,
    )
```

```python
import functools

import jax
import jax.numpy as jnp
from jax import lax
from jax.experimental import pallas as pl
from jax.experimental.pallas import tpu as pltpu
from jax.sharding import PartitionSpec as P

BLK = 128
LEVELS = 32767.0
TINY = 1e-33
MESH = pl.DeviceIdType.MESH


def times_flag(block, flag):
    scale = jnp.full(block.shape, flag.astype(jnp.float32)).astype(block.dtype)
    return block * scale


def kernel(
    group, parts,
    a_hbm, b_hbm, mask_a, mask_b, out_tile,
    flags_a, flags_b, a_tile, b_own, b_send, b_recv, own_sum, code_send, code_recv, step_send, step_recv,
    f_sem, a_sem, b_sem, bs_sem, br_sem, cs_sem, cr_sem, ss_sem, sr_sem,
):
    n_row, n_col = lax.axis_size("row"), lax.axis_size("col")
    row, col = lax.axis_index("row"), lax.axis_index("col")
    up, down = lax.rem(row + n_row - 1, n_row), lax.rem(row + 1, n_row)
    left, right = lax.rem(col + n_col - 1, n_col), lax.rem(col + 1, n_col)
    rows, inner = a_tile.shape
    width = b_own.shape[1]
    deep, halves = inner // BLK, width // BLK
    span = group * BLK
    chunks = rows // span
    cut = inner // parts

    def piece(c):
        return pl.ds(pl.multiple_of(c * span, span), span)

    def load_a(c):
        return pltpu.make_async_copy(a_hbm.at[piece(c), :], a_tile.at[piece(c), :], a_sem.at[c])

    slot = jnp.where(row == 0, 1, 0)

    def load_send(n):
        h, p = divmod(n, parts)
        return pltpu.make_async_copy(
            b_hbm.at[pl.ds(pl.multiple_of(slot * inner + p * cut, cut), cut), h * BLK:(h + 1) * BLK],
            b_send.at[h, p * cut:(p + 1) * cut, :], b_sem.at[n],
        )

    get_own = pltpu.make_async_copy(b_hbm.at[pl.ds(0, inner), :], b_own, b_sem.at[halves * parts])

    barrier = pltpu.get_barrier_semaphore()
    pl.semaphore_signal(barrier, inc=1, device_id={"row": down, "col": left}, device_id_type=MESH)
    pl.semaphore_signal(barrier, inc=1, device_id={"row": down, "col": col}, device_id_type=MESH)
    get_flags_b = pltpu.make_async_copy(mask_b, flags_b, f_sem.at[0])
    get_flags_a = pltpu.make_async_copy(mask_a, flags_a, f_sem.at[1])
    get_flags_b.start()
    for n in range(halves * parts):
        load_send(n).start()
    get_flags_a.start()
    get_own.start()
    for c in range(chunks):
        load_a(c).start()

    def move_b(n):
        h, p = divmod(n, parts)
        spot = (h, slice(p * cut, (p + 1) * cut))
        return pltpu.make_async_remote_copy(
            src_ref=b_send.at[spot], dst_ref=b_recv.at[spot], send_sem=bs_sem.at[n], recv_sem=br_sem.at[n],
            device_id={"row": up, "col": right}, device_id_type=MESH,
        )

    get_flags_b.wait()
    for n in range(halves * parts):
        load_send(n).wait()
        h, p = divmod(n, parts)
        for k in range(p * deep // parts, (p + 1) * deep // parts):
            lines = slice(k * BLK, (k + 1) * BLK)
            b_send[h, lines, :] = times_flag(b_send[h, lines, :], flags_b[h, slot * deep + k])
        if n == 0:
            pl.semaphore_wait(barrier, 2)
        move_b(n).start()

    get_own.wait()
    for h in range(halves):
        for k in range(deep):
            spot = (slice(k * BLK, (k + 1) * BLK), slice(h * BLK, (h + 1) * BLK))
            b_own[spot] = times_flag(b_own[spot], flags_b[h, k])

    def own_part(c, carry):
        load_a(c).wait()
        for g in range(group):
            lines = pl.ds(pl.multiple_of(c * span + g * BLK, BLK), BLK)
            for k in range(deep):
                block = a_tile[lines, k * BLK:(k + 1) * BLK]
                a_tile[lines, k * BLK:(k + 1) * BLK] = times_flag(block, flags_a[k, c * group + g])
        own_sum[piece(c), :] = jnp.dot(a_tile[piece(c), :], b_own[...], preferred_element_type=jnp.float32)
        return carry

    get_flags_a.wait()
    lax.fori_loop(0, chunks, own_part, 0)

    def move_code(i):
        return pltpu.make_async_remote_copy(
            src_ref=code_send.at[i], dst_ref=code_recv.at[i], send_sem=cs_sem.at[i], recv_sem=cr_sem.at[i],
            device_id={"row": row, "col": left}, device_id_type=MESH,
        )

    def move_step(i):
        return pltpu.make_async_remote_copy(
            src_ref=step_send.at[i], dst_ref=step_recv.at[i], send_sem=ss_sem.at[i], recv_sem=sr_sem.at[i],
            device_id={"row": row, "col": left}, device_id_type=MESH,
        )

    def send_out(i, carry):
        move_step(i).start()
        move_code(i).start()
        return carry

    def next_part(h, early, c, carry):
        i = h * chunks + c
        value = jnp.dot(a_tile[piece(c), :], b_recv[h], preferred_element_type=jnp.float32)
        most = jnp.maximum(jnp.max(jnp.abs(value), axis=0, keepdims=True), TINY)
        step_send[i] = jnp.broadcast_to(most * (1.0 / LEVELS), step_send.shape[1:])
        code_send[i] = jnp.round(value * (LEVELS / most)).astype(jnp.int32).astype(jnp.int16)
        return carry if early else send_out(i, carry)

    for h in range(halves):
        for n in range(h * parts, (h + 1) * parts):
            move_b(n).wait_recv()
        if h == halves - 1:
            pass
        lax.fori_loop(0, chunks, functools.partial(next_part, h, h < halves - 1), 0)
        if h == halves - 2:
            for n in range(halves * parts):
                move_b(n).wait_send()
            lax.fori_loop(0, (halves - 1) * chunks, send_out, 0)

    for h in range(halves):

        def finish(c, carry, h=h):
            i = h * chunks + c
            move_step(i).wait_recv()
            move_code(i).wait_recv()
            code = code_recv[i].astype(jnp.int32).astype(jnp.float32)
            total = own_sum[piece(c), h * BLK:(h + 1) * BLK] + code * step_recv[i, 0:1, :]
            out_tile[piece(c), h * BLK:(h + 1) * BLK] = total.astype(out_tile.dtype)
            return carry

        lax.fori_loop(0, chunks, finish, 0)

    pass

    for n in range(halves * parts, halves * parts):
        move_b(n).wait_send()

    def sent(i, carry):
        move_step(i).wait_send()
        move_code(i).wait_send()
        return carry

    lax.fori_loop(0, halves * chunks, sent, 0)


def hand_on(pieces, source, target, held, in_sem, out_sem):
    span = source.shape[0] // pieces

    def fetch(n):
        return pltpu.make_async_copy(source.at[n * span:(n + 1) * span, :], held.at[n], in_sem.at[n])

    def put(n):
        return pltpu.make_async_copy(held.at[n], target.at[n * span:(n + 1) * span, :], out_sem.at[n])

    for n in range(pieces):
        fetch(n).start()
    for n in range(pieces):
        fetch(n).wait()
        put(n).start()
    for n in range(pieces):
        put(n).wait()


def pass_on(pieces, source, target, sem):
    span = source.shape[0] // pieces

    def put(n):
        return pltpu.make_async_copy(source.at[n * span:(n + 1) * span, :], target.at[n * span:(n + 1) * span, :], sem.at[n])

    for n in range(pieces):
        put(n).start()
    for n in range(pieces):
        put(n).wait()


def body(mat_a, mat_b, mask_a, mask_b):
    rows, inner = mat_a.shape
    width = mat_b.shape[1]
    block_rows = mask_a.shape[0]
    group = next(g for g in (4, 2, 1) if block_rows % g == 0)
    span = group * BLK
    chunks = rows // span
    halves = width // BLK
    sends = halves * chunks
    deep = inner // BLK
    parts = next(p for p in (4, 3, 2, 1) if deep % p == 0)
    dma = pltpu.SemaphoreType.DMA
    product = pl.pallas_call(
        functools.partial(kernel, group, parts),
        out_shape=pltpu.VMEM((rows, width), jnp.bfloat16),
        in_specs=[
            pl.BlockSpec(memory_space=pl.ANY),
            pl.BlockSpec(memory_space=pl.ANY),
            pl.BlockSpec(memory_space=pl.ANY),
            pl.BlockSpec(memory_space=pl.ANY),
        ],
        out_specs=pl.BlockSpec(memory_space=pltpu.VMEM),
        scratch_shapes=[
            pltpu.SMEM(mask_a.shape[::-1], jnp.int32),
            pltpu.SMEM(mask_b.shape[::-1], jnp.int32),
            pltpu.VMEM((rows, inner), jnp.bfloat16),
            pltpu.VMEM((inner, width), jnp.bfloat16),
            pltpu.VMEM((halves, inner, BLK), jnp.bfloat16),
            pltpu.VMEM((halves, inner, BLK), jnp.bfloat16),
            pltpu.VMEM((rows, width), jnp.float32),
            pltpu.VMEM((sends, span, BLK), jnp.int16),
            pltpu.VMEM((sends, span, BLK), jnp.int16),
            pltpu.VMEM((sends, 8, BLK), jnp.float32),
            pltpu.VMEM((sends, 8, BLK), jnp.float32),
            dma((2,)), dma((chunks,)), dma((halves * parts + 1,)), dma((halves * parts,)), dma((halves * parts,)),
            dma((sends,)), dma((sends,)), dma((sends,)), dma((sends,)),
        ],
        compiler_params=pltpu.CompilerParams(collective_id=0, has_side_effects=True, vmem_limit_bytes=55 * 1000 * 1000),
        name="cannon",
    )(mat_a, mat_b, pltpu.with_memory_space_constraint(mask_a.T, pltpu.MemorySpace.HBM), pltpu.with_memory_space_constraint(mask_b.T, pltpu.MemorySpace.HBM))
    return pl.pallas_call(
        functools.partial(pass_on, chunks),
        out_shape=jax.ShapeDtypeStruct(product.shape, product.dtype),
        in_specs=[pl.BlockSpec(memory_space=pl.ANY)],
        out_specs=pl.BlockSpec(memory_space=pl.ANY),
        scratch_shapes=[dma((chunks,))],
        compiler_params=pltpu.CompilerParams(vmem_limit_bytes=1024 * 1024),
        name="pass_on",
    )(product)


def solution(mesh):
    return jax.shard_map(
        body,
        mesh=mesh,
        in_specs=(P("row", "col"), P("row", "col"), P("row", "col"), P("row", "col")),
        out_specs=P("row", "col"),
        check_vma=False,
    )
```

```python
import functools

import jax
import jax.numpy as jnp
from jax import lax
from jax.experimental import pallas as pl
from jax.experimental.pallas import tpu as pltpu
from jax.sharding import PartitionSpec as P

BLK = 128
LEVELS = 32767.0
TINY = 1e-33
B_WINDOW = 3
R_WINDOW = 3
B_PARTS = (4, 3, 2, 1)
MESH = pl.DeviceIdType.MESH


def times_flag(block, flag):
    scale = jnp.full(block.shape, flag.astype(jnp.float32)).astype(block.dtype)
    return block * scale


def kernel(
    group, parts,
    a_hbm, b_hbm, mask_a, mask_b, out_tile,
    flags_a, flags_b, a_tile, b_own, b_send, b_recv, own_sum, code_send, code_recv, step_send, step_recv,
    f_sem, a_sem, b_sem, bs_sem, br_sem, cs_sem, cr_sem, ss_sem, sr_sem,
):
    n_row, n_col = lax.axis_size("row"), lax.axis_size("col")
    row, col = lax.axis_index("row"), lax.axis_index("col")
    up, down = lax.rem(row + n_row - 1, n_row), lax.rem(row + 1, n_row)
    left, right = lax.rem(col + n_col - 1, n_col), lax.rem(col + 1, n_col)
    rows, inner = a_tile.shape
    width = b_own.shape[1]
    deep, halves = inner // BLK, width // BLK
    span = group * BLK
    chunks = rows // span
    cut = inner // parts
    pieces, sends = halves * parts, halves * chunks
    ready = sends - chunks
    b_window, r_window = min(B_WINDOW, pieces), min(R_WINDOW, ready)

    def lines_of(c):
        return pl.ds(pl.multiple_of(c * span, span), span)

    def load_a(c):
        return pltpu.make_async_copy(a_hbm.at[lines_of(c), :], a_tile.at[lines_of(c), :], a_sem.at[c])

    slot = jnp.where(row == 0, 1, 0)

    def load_send(n):
        h, p = divmod(n, parts)
        return pltpu.make_async_copy(
            b_hbm.at[pl.ds(pl.multiple_of(slot * inner + p * cut, cut), cut), h * BLK:(h + 1) * BLK], b_send.at[n], b_sem.at[n]
        )

    get_own = pltpu.make_async_copy(b_hbm.at[pl.ds(0, inner), :], b_own, b_sem.at[pieces])
    get_flags_b = pltpu.make_async_copy(mask_b, flags_b, f_sem.at[0])
    get_flags_a = pltpu.make_async_copy(mask_a, flags_a, f_sem.at[1])

    def move_b(n):
        return pltpu.make_async_remote_copy(
            src_ref=b_send.at[n], dst_ref=b_recv.at[n], send_sem=bs_sem.at[n], recv_sem=br_sem.at[n],
            device_id={"row": up, "col": right}, device_id_type=MESH,
        )

    def move_code(i):
        return pltpu.make_async_remote_copy(
            src_ref=code_send.at[i], dst_ref=code_recv.at[i], send_sem=cs_sem.at[i], recv_sem=cr_sem.at[i],
            device_id={"row": row, "col": left}, device_id_type=MESH,
        )

    def move_step(i):
        return pltpu.make_async_remote_copy(
            src_ref=step_send.at[i], dst_ref=step_recv.at[i], send_sem=ss_sem.at[i], recv_sem=sr_sem.at[i],
            device_id={"row": row, "col": left}, device_id_type=MESH,
        )

    barrier = pltpu.get_barrier_semaphore()
    pl.semaphore_signal(barrier, inc=1, device_id={"row": down, "col": left}, device_id_type=MESH)
    pl.semaphore_signal(barrier, inc=1, device_id={"row": down, "col": col}, device_id_type=MESH)
    get_flags_b.start()
    for n in range(pieces):
        load_send(n).start()
    get_flags_b.wait()
    for n in range(pieces):
        load_send(n).wait()
        h, p = divmod(n, parts)
        for k in range(deep // parts):
            lines = slice(k * BLK, (k + 1) * BLK)
            b_send[n, lines, :] = times_flag(b_send[n, lines, :], flags_b[h, slot * deep + p * (deep // parts) + k])
        if n == 0:
            pl.semaphore_wait(barrier, 2)
        if n < b_window:
            move_b(n).start()
        if n == 0:
            get_flags_a.start()
            get_own.start()
            for c in range(chunks):
                load_a(c).start()

    get_own.wait()
    for h in range(halves):
        for k in range(deep):
            spot = (slice(k * BLK, (k + 1) * BLK), slice(h * BLK, (h + 1) * BLK))
            b_own[spot] = times_flag(b_own[spot], flags_b[h, k])
    get_flags_a.wait()

    def next_b(n, carry):
        move_b(n - b_window).wait_send()
        move_b(n).start()
        return carry

    def own_part(c, carry):
        load_a(c).wait()
        for g in range(group):
            lines = pl.ds(pl.multiple_of(c * span + g * BLK, BLK), BLK)
            for k in range(deep):
                block = a_tile[lines, k * BLK:(k + 1) * BLK]
                a_tile[lines, k * BLK:(k + 1) * BLK] = times_flag(block, flags_a[k, c * group + g])
        own_sum[lines_of(c), :] = jnp.dot(a_tile[lines_of(c), :], b_own[...], preferred_element_type=jnp.float32)

        @pl.when(b_window + c < pieces)
        def _():
            next_b(b_window + c, 0)

        return carry

    lax.fori_loop(0, chunks, own_part, 0)
    lax.fori_loop(min(b_window + chunks, pieces), pieces, next_b, 0)

    def send_out(i, carry):
        move_step(i).start()
        move_code(i).start()
        return carry

    def sent(i, carry):
        move_step(i).wait_send()
        move_code(i).wait_send()
        return carry

    def next_out(i, carry):
        sent(i - r_window, carry)
        return send_out(i, carry)

    def next_part(h, c, carry):
        i = h * chunks + c
        tile = b_recv[h * parts:(h + 1) * parts].reshape(inner, BLK)
        value = jnp.dot(a_tile[lines_of(c), :], tile, preferred_element_type=jnp.float32)
        most = jnp.maximum(jnp.max(jnp.abs(value), axis=0, keepdims=True), TINY)
        step_send[i] = most * (1.0 / LEVELS)
        code_send[i] = jnp.round(value * (LEVELS / most)).astype(jnp.int32).astype(jnp.int16)
        if h < halves - 1:
            return carry
        return next_out(r_window + c, carry) if r_window else send_out(c, carry)

    for h in range(halves):
        if h == halves - 1:
            for n in range(pieces - b_window, pieces):
                move_b(n).wait_send()
            lax.fori_loop(0, r_window, send_out, 0)
        for n in range(h * parts, (h + 1) * parts):
            move_b(n).wait_recv()
        lax.fori_loop(0, chunks, functools.partial(next_part, h), 0)
    if r_window:
        lax.fori_loop(r_window + chunks, sends, next_out, 0)

    for h in range(halves):

        def finish(c, carry, h=h):
            i = h * chunks + c
            move_step(i).wait_recv()
            move_code(i).wait_recv()
            code = code_recv[i].astype(jnp.int32).astype(jnp.float32)
            total = own_sum[lines_of(c), h * BLK:(h + 1) * BLK] + code * step_recv[i]
            out_tile[lines_of(c), h * BLK:(h + 1) * BLK] = total.astype(out_tile.dtype)
            return carry

        lax.fori_loop(0, chunks, finish, 0)
    lax.fori_loop(sends - r_window if r_window else 0, sends, sent, 0)


def pass_on(pieces, source, target, sem):
    span = source.shape[0] // pieces

    def put(n):
        return pltpu.make_async_copy(source.at[n * span:(n + 1) * span, :], target.at[n * span:(n + 1) * span, :], sem.at[n])

    for n in range(pieces):
        put(n).start()
    for n in range(pieces):
        put(n).wait()


def in_hbm(array):
    return pltpu.with_memory_space_constraint(array, pltpu.MemorySpace.HBM)


def body(mat_a, mat_b, mask_a, mask_b):
    rows, inner = mat_a.shape
    width = mat_b.shape[1]
    block_rows = mask_a.shape[0]
    group = next(g for g in (4, 2, 1) if block_rows % g == 0)
    parts = next(p for p in B_PARTS if inner // BLK % p == 0)
    span = group * BLK
    chunks = rows // span
    halves = width // BLK
    pieces, sends = halves * parts, halves * chunks
    dma = pltpu.SemaphoreType.DMA
    product = pl.pallas_call(
        functools.partial(kernel, group, parts),
        out_shape=pltpu.VMEM((rows, width), jnp.bfloat16),
        in_specs=[pl.BlockSpec(memory_space=pl.ANY)] * 4,
        out_specs=pl.BlockSpec(memory_space=pltpu.VMEM),
        scratch_shapes=[
            pltpu.SMEM(mask_a.shape[::-1], jnp.int32),
            pltpu.SMEM(mask_b.shape[::-1], jnp.int32),
            pltpu.VMEM((rows, inner), jnp.bfloat16),
            pltpu.VMEM((inner, width), jnp.bfloat16),
            pltpu.VMEM((pieces, inner // parts, BLK), jnp.bfloat16),
            pltpu.VMEM((pieces, inner // parts, BLK), jnp.bfloat16),
            pltpu.VMEM((rows, width), jnp.float32),
            pltpu.VMEM((sends, span, BLK), jnp.int16),
            pltpu.VMEM((sends, span, BLK), jnp.int16),
            pltpu.VMEM((sends, 1, BLK), jnp.float32),
            pltpu.VMEM((sends, 1, BLK), jnp.float32),
            dma((2,)), dma((chunks,)), dma((pieces + 1,)), dma((pieces,)), dma((pieces,)),
            dma((sends,)), dma((sends,)), dma((sends,)), dma((sends,)),
        ],
        compiler_params=pltpu.CompilerParams(collective_id=0, has_side_effects=True, vmem_limit_bytes=52 * 1024 * 1024),
        name="cannon",
    )(mat_a, mat_b, in_hbm(mask_a.T), in_hbm(mask_b.T))
    return pl.pallas_call(
        functools.partial(pass_on, chunks),
        out_shape=jax.ShapeDtypeStruct(product.shape, product.dtype),
        in_specs=[pl.BlockSpec(memory_space=pl.ANY)],
        out_specs=pl.BlockSpec(memory_space=pl.ANY),
        scratch_shapes=[dma((chunks,))],
        compiler_params=pltpu.CompilerParams(vmem_limit_bytes=1024 * 1024),
        name="pass_on",
    )(product)


def solution(mesh):
    return jax.shard_map(
        body,
        mesh=mesh,
        in_specs=(P("row", "col"), P("row", "col"), P("row", "col"), P("row", "col")),
        out_specs=P("row", "col"),
        check_vma=False,
    )
```

```python
import functools

import jax
import jax.numpy as jnp
from jax import lax
from jax.experimental import pallas as pl
from jax.experimental.pallas import tpu as pltpu
from jax.sharding import PartitionSpec as P

BLK = 128
LEVELS = 32767.0
TINY = 1e-33
PLANE = 4
B_WINDOW = 3
R_WINDOW = 3
B_PARTS = (6, 4, 3, 2, 1)
MESH = pl.DeviceIdType.MESH


def times_flag(block, flag):
    scale = jnp.full(block.shape, flag.astype(jnp.float32)).astype(block.dtype)
    return block * scale


def kernel(
    group, parts,
    a_hbm, b_hbm, mask_a, mask_b, out_tile,
    flags_a, flags_b, a_tile, b_own, b_send, b_recv, own_sum, code_send, code_recv, step_send, step_recv, passing,
    f_sem, a_sem, b_sem, bs_sem, br_sem, cs_sem, cr_sem, ss_sem, sr_sem, p_sem,
):
    n_row, n_col = lax.axis_size("row"), lax.axis_size("col")
    row, col = lax.axis_index("row"), lax.axis_index("col")
    up, down = lax.rem(row + n_row - 1, n_row), lax.rem(row + 1, n_row)
    left, right = lax.rem(col + n_col - 1, n_col), lax.rem(col + 1, n_col)
    rows, inner = a_tile.shape
    width = b_own.shape[1]
    deep, halves = inner // BLK, width // BLK
    span = group * BLK
    chunks = rows // span
    cut = inner // parts
    pieces, sends = halves * parts, halves * chunks
    ready = sends - chunks
    b_window, r_window = min(B_WINDOW, pieces), min(R_WINDOW, ready)

    def lines_of(c):
        return pl.ds(pl.multiple_of(c * span, span), span)

    def load_a(c):
        return pltpu.make_async_copy(a_hbm.at[lines_of(c), :], a_tile.at[lines_of(c), :], a_sem.at[c])

    slot = jnp.where(row == 0, 1, 0)

    def load_send(n):
        h, p = divmod(n, parts)
        return pltpu.make_async_copy(
            b_hbm.at[pl.ds(pl.multiple_of(slot * inner + p * cut, cut), cut), h * BLK:(h + 1) * BLK], b_send.at[n], b_sem.at[n]
        )

    get_own = pltpu.make_async_copy(b_hbm.at[pl.ds(0, inner), :], b_own, b_sem.at[pieces])
    get_flags_b = pltpu.make_async_copy(mask_b, flags_b, f_sem.at[0])
    get_flags_a = pltpu.make_async_copy(mask_a, flags_a, f_sem.at[1])

    def move_b(n):
        return pltpu.make_async_remote_copy(
            src_ref=b_send.at[n], dst_ref=b_recv.at[n], send_sem=bs_sem.at[n], recv_sem=br_sem.at[n],
            device_id={"row": up, "col": right}, device_id_type=MESH,
        )

    def move_code(i):
        return pltpu.make_async_remote_copy(
            src_ref=code_send.at[i], dst_ref=code_recv.at[i], send_sem=cs_sem.at[i], recv_sem=cr_sem.at[i],
            device_id={"row": row, "col": left}, device_id_type=MESH,
        )

    def move_step(i):
        return pltpu.make_async_remote_copy(
            src_ref=step_send.at[i], dst_ref=step_recv.at[i], send_sem=ss_sem.at[i], recv_sem=sr_sem.at[i],
            device_id={"row": row, "col": left}, device_id_type=MESH,
        )

    last_col, last_piece = n_col - 1, pieces - 1
    relay = max(n_col - 2, 0)
    hand_over = pltpu.make_async_remote_copy(
        src_ref=b_send.at[last_piece], dst_ref=passing, send_sem=bs_sem.at[last_piece], recv_sem=p_sem.at[0],
        device_id={"row": up, "col": relay}, device_id_type=MESH,
    )
    pass_along = pltpu.make_async_remote_copy(
        src_ref=passing, dst_ref=b_recv.at[last_piece], send_sem=p_sem.at[1], recv_sem=br_sem.at[last_piece],
        device_id={"row": row, "col": 0}, device_id_type=MESH,
    )

    barrier = pltpu.get_barrier_semaphore()
    pl.semaphore_signal(barrier, inc=1, device_id={"row": down, "col": left}, device_id_type=MESH)
    pl.semaphore_signal(barrier, inc=1, device_id={"row": down, "col": col}, device_id_type=MESH)

    @pl.when(col == 0)
    def _():
        pl.semaphore_signal(barrier, inc=1, device_id={"row": row, "col": relay}, device_id_type=MESH)

    @pl.when(col == relay)
    def _():
        pl.semaphore_signal(barrier, inc=1, device_id={"row": down, "col": last_col}, device_id_type=MESH)

    get_flags_b.start()
    for n in range(pieces):
        load_send(n).start()
    get_flags_b.wait()
    for n in range(pieces):
        load_send(n).wait()
        h, p = divmod(n, parts)
        for k in range(deep // parts):
            lines = slice(k * BLK, (k + 1) * BLK)
            b_send[n, lines, :] = times_flag(b_send[n, lines, :], flags_b[h, slot * deep + p * (deep // parts) + k])
        if n == 0:
            pl.semaphore_wait(barrier, 2 + jnp.where(col == last_col, 1, 0) + jnp.where(col == relay, 1, 0))
        if n < b_window:
            move_b(n).start()
        if n == 0:
            get_flags_a.start()
            get_own.start()
            for c in range(chunks):
                load_a(c).start()


    @pl.when(col == last_col)
    def _():
        hand_over.start()

    get_own.wait()
    for h in range(halves):
        for k in range(deep):
            spot = (slice(k * BLK, (k + 1) * BLK), slice(h * BLK, (h + 1) * BLK))
            b_own[spot] = times_flag(b_own[spot], flags_b[h, k])
    get_flags_a.wait()

    def next_b(n, carry):
        move_b(n - b_window).wait_send()

        @pl.when((col != last_col) | (n != last_piece))
        def _():
            move_b(n).start()

        return carry

    def own_part(c, carry):
        load_a(c).wait()
        for g in range(group):
            lines = pl.ds(pl.multiple_of(c * span + g * BLK, BLK), BLK)
            for k in range(deep):
                block = a_tile[lines, k * BLK:(k + 1) * BLK]
                a_tile[lines, k * BLK:(k + 1) * BLK] = times_flag(block, flags_a[k, c * group + g])
        own_sum[lines_of(c), :] = jnp.dot(a_tile[lines_of(c), :], b_own[...], preferred_element_type=jnp.float32)

        @pl.when(b_window + c < pieces)
        def _():
            next_b(b_window + c, 0)

        return carry

    lax.fori_loop(0, chunks, own_part, 0)
    lax.fori_loop(min(b_window + chunks, pieces), pieces, next_b, 0)

    def send_out(i, carry):
        move_step(i).start()
        move_code(i).start()
        return carry

    def sent(i, carry):
        move_step(i).wait_send()
        move_code(i).wait_send()
        return carry

    def next_out(i, carry):
        sent(i - r_window, carry)
        return send_out(i, carry)

    def next_part(h, c, carry):
        i = h * chunks + c
        tile = b_recv[h * parts:(h + 1) * parts].reshape(inner, BLK)
        value = jnp.dot(a_tile[lines_of(c), :], tile, preferred_element_type=jnp.float32)
        most = jnp.maximum(jnp.max(jnp.abs(value), axis=0, keepdims=True), TINY)
        step_send[i] = most * (1.0 / LEVELS)
        code_send[i] = jnp.round(value * (LEVELS / most)).astype(jnp.int32).astype(jnp.int16)
        if h < halves - 1:
            return carry
        return next_out(r_window + c, carry) if r_window else send_out(c, carry)

    for h in range(halves):
        if h == halves - 1:
            hold = (lax.rem(col, PLANE) == 0) | (col == relay)

            @pl.when(jnp.logical_not(hold))
            def _():
                lax.fori_loop(0, r_window, send_out, 0)

            for n in range(pieces - b_window, pieces):
                move_b(n).wait_send()

            @pl.when(hold)
            def _():
                lax.fori_loop(0, 1, send_out, 0)

            @pl.when(col == relay)
            def _():
                hand_over.wait_recv()
                pass_along.start()

            @pl.when(hold)
            def _():
                lax.fori_loop(1, r_window, send_out, 0)

        for n in range(h * parts, (h + 1) * parts):
            move_b(n).wait_recv()
        lax.fori_loop(0, chunks, functools.partial(next_part, h), 0)
    if r_window:
        lax.fori_loop(r_window + chunks, sends, next_out, 0)

    for h in range(halves):

        def finish(c, carry, h=h):
            i = h * chunks + c
            move_step(i).wait_recv()
            move_code(i).wait_recv()
            code = code_recv[i].astype(jnp.int32).astype(jnp.float32)
            total = own_sum[lines_of(c), h * BLK:(h + 1) * BLK] + code * step_recv[i]
            out_tile[lines_of(c), h * BLK:(h + 1) * BLK] = total.astype(out_tile.dtype)
            return carry

        lax.fori_loop(0, chunks, finish, 0)
    lax.fori_loop(sends - r_window if r_window else 0, sends, sent, 0)

    @pl.when(col == relay)
    def _():
        pass_along.wait_send()


def pass_on(pieces, source, target, sem):
    span = source.shape[0] // pieces

    def put(n):
        return pltpu.make_async_copy(source.at[n * span:(n + 1) * span, :], target.at[n * span:(n + 1) * span, :], sem.at[n])

    for n in range(pieces):
        put(n).start()
    for n in range(pieces):
        put(n).wait()


def in_hbm(array):
    return pltpu.with_memory_space_constraint(array, pltpu.MemorySpace.HBM)


def body(mat_a, mat_b, mask_a, mask_b):
    rows, inner = mat_a.shape
    width = mat_b.shape[1]
    block_rows = mask_a.shape[0]
    group = next(g for g in (4, 2, 1) if block_rows % g == 0)
    parts = next(p for p in B_PARTS if inner // BLK % p == 0)
    span = group * BLK
    chunks = rows // span
    halves = width // BLK
    pieces, sends = halves * parts, halves * chunks
    dma = pltpu.SemaphoreType.DMA
    product = pl.pallas_call(
        functools.partial(kernel, group, parts),
        out_shape=pltpu.VMEM((rows, width), jnp.bfloat16),
        in_specs=[pl.BlockSpec(memory_space=pl.ANY)] * 4,
        out_specs=pl.BlockSpec(memory_space=pltpu.VMEM),
        scratch_shapes=[
            pltpu.SMEM(mask_a.shape[::-1], jnp.int32),
            pltpu.SMEM(mask_b.shape[::-1], jnp.int32),
            pltpu.VMEM((rows, inner), jnp.bfloat16),
            pltpu.VMEM((inner, width), jnp.bfloat16),
            pltpu.VMEM((pieces, inner // parts, BLK), jnp.bfloat16),
            pltpu.VMEM((pieces, inner // parts, BLK), jnp.bfloat16),
            pltpu.VMEM((rows, width), jnp.float32),
            pltpu.VMEM((sends, span, BLK), jnp.int16),
            pltpu.VMEM((sends, span, BLK), jnp.int16),
            pltpu.VMEM((sends, 1, BLK), jnp.float32),
            pltpu.VMEM((sends, 1, BLK), jnp.float32),
            pltpu.VMEM((inner // parts, BLK), jnp.bfloat16),
            dma((2,)), dma((chunks,)), dma((pieces + 1,)), dma((pieces,)), dma((pieces,)),
            dma((sends,)), dma((sends,)), dma((sends,)), dma((sends,)), dma((2,)),
        ],
        compiler_params=pltpu.CompilerParams(collective_id=0, has_side_effects=True, vmem_limit_bytes=52 * 1024 * 1024),
        name="cannon",
    )(mat_a, mat_b, in_hbm(mask_a.T), in_hbm(mask_b.T))
    return pl.pallas_call(
        functools.partial(pass_on, chunks),
        out_shape=jax.ShapeDtypeStruct(product.shape, product.dtype),
        in_specs=[pl.BlockSpec(memory_space=pl.ANY)],
        out_specs=pl.BlockSpec(memory_space=pl.ANY),
        scratch_shapes=[dma((chunks,))],
        compiler_params=pltpu.CompilerParams(vmem_limit_bytes=1024 * 1024),
        name="pass_on",
    )(product)


def solution(mesh):
    return jax.shard_map(
        body,
        mesh=mesh,
        in_specs=(P("row", "col"), P("row", "col"), P("row", "col"), P("row", "col")),
        out_specs=P("row", "col"),
        check_vma=False,
    )
```

```python
import functools

import jax
import jax.numpy as jnp
from jax import lax
from jax.experimental import pallas as pl
from jax.experimental.pallas import tpu as pltpu
from jax.sharding import PartitionSpec as P

BLK = 128
LEVELS = 32767.0
TINY = 1e-33
PLANE = 4
B_PARTS = (6, 4, 3, 2, 1)
MESH = pl.DeviceIdType.MESH


def runs(start, sizes):
    found = []
    for size in sizes:
        if size > 0:
            found.append((start, size))
        start += size
    return found


def b_runs(halves, parts):
    found = []
    for h in range(halves - 1):
        found += runs(h * parts, (parts // 2, parts - parts // 2))
    return found + runs((halves - 1) * parts, (parts - 1, 1))


def r_runs(halves, chunks):
    first = max(2 * chunks // 5, 1)
    found = []
    for h in range(halves - 1):
        found += runs(h * chunks, (first, chunks - first))
    return found, runs((halves - 1) * chunks, (chunks - 1, 1))


def times_flag(block, flag):
    scale = jnp.full(block.shape, flag.astype(jnp.float32)).astype(block.dtype)
    return block * scale


def kernel(
    group, parts,
    a_hbm, b_hbm, mask_a, mask_b, out_tile,
    flags_a, flags_b, a_tile, b_own, b_send, b_recv, own_sum, code_send, code_recv, step_send, step_recv, passing,
    f_sem, a_sem, b_sem, bs_sem, br_sem, cs_sem, cr_sem, ss_sem, sr_sem, p_sem,
):
    n_row, n_col = lax.axis_size("row"), lax.axis_size("col")
    row, col = lax.axis_index("row"), lax.axis_index("col")
    up, down = lax.rem(row + n_row - 1, n_row), lax.rem(row + 1, n_row)
    left, right = lax.rem(col + n_col - 1, n_col), lax.rem(col + 1, n_col)
    rows, inner = a_tile.shape
    width = b_own.shape[1]
    deep, halves = inner // BLK, width // BLK
    span = group * BLK
    chunks = rows // span
    cut = inner // parts
    pieces, sends = halves * parts, halves * chunks
    b_parts, (r_early, r_late) = b_runs(halves, parts), r_runs(halves, chunks)
    r_parts = r_early + r_late

    def lines_of(c):
        return pl.ds(pl.multiple_of(c * span, span), span)

    def load_a(c):
        return pltpu.make_async_copy(a_hbm.at[lines_of(c), :], a_tile.at[lines_of(c), :], a_sem.at[c])

    slot = jnp.where(row == 0, 1, 0)

    def load_send(n):
        h, p = divmod(n, parts)
        return pltpu.make_async_copy(
            b_hbm.at[pl.ds(pl.multiple_of(slot * inner + p * cut, cut), cut), h * BLK:(h + 1) * BLK], b_send.at[n], b_sem.at[n]
        )

    get_own = pltpu.make_async_copy(b_hbm.at[pl.ds(0, inner), :], b_own, b_sem.at[pieces])
    get_flags_b = pltpu.make_async_copy(mask_b, flags_b, f_sem.at[0])
    get_flags_a = pltpu.make_async_copy(mask_a, flags_a, f_sem.at[1])

    def move_b(j):
        start, size = b_parts[j]
        spot = slice(start, start + size)
        return pltpu.make_async_remote_copy(
            src_ref=b_send.at[spot], dst_ref=b_recv.at[spot], send_sem=bs_sem.at[j], recv_sem=br_sem.at[j],
            device_id={"row": up, "col": right}, device_id_type=MESH,
        )

    def move_code(j):
        start, size = r_parts[j]
        spot = slice(start, start + size)
        return pltpu.make_async_remote_copy(
            src_ref=code_send.at[spot], dst_ref=code_recv.at[spot], send_sem=cs_sem.at[j], recv_sem=cr_sem.at[j],
            device_id={"row": row, "col": left}, device_id_type=MESH,
        )

    def move_step(h):
        spot = slice(h * chunks, (h + 1) * chunks)
        return pltpu.make_async_remote_copy(
            src_ref=step_send.at[spot], dst_ref=step_recv.at[spot], send_sem=ss_sem.at[h], recv_sem=sr_sem.at[h],
            device_id={"row": row, "col": left}, device_id_type=MESH,
        )

    last_col, last_part = n_col - 1, len(b_parts) - 1
    tail = slice(b_parts[-1][0], pieces)
    relay = max(n_col - 2, 0)
    hand_over = pltpu.make_async_remote_copy(
        src_ref=b_send.at[tail], dst_ref=passing, send_sem=bs_sem.at[last_part], recv_sem=p_sem.at[0],
        device_id={"row": up, "col": relay}, device_id_type=MESH,
    )
    pass_along = pltpu.make_async_remote_copy(
        src_ref=passing, dst_ref=b_recv.at[tail], send_sem=p_sem.at[1], recv_sem=br_sem.at[last_part],
        device_id={"row": row, "col": 0}, device_id_type=MESH,
    )

    barrier = pltpu.get_barrier_semaphore()
    pl.semaphore_signal(barrier, inc=1, device_id={"row": down, "col": left}, device_id_type=MESH)
    pl.semaphore_signal(barrier, inc=1, device_id={"row": down, "col": col}, device_id_type=MESH)

    @pl.when(col == 0)
    def _():
        pl.semaphore_signal(barrier, inc=1, device_id={"row": row, "col": relay}, device_id_type=MESH)

    @pl.when(col == relay)
    def _():
        pl.semaphore_signal(barrier, inc=1, device_id={"row": down, "col": last_col}, device_id_type=MESH)

    get_flags_b.start()
    for n in range(pieces):
        load_send(n).start()
    get_flags_b.wait()
    for n in range(pieces):
        load_send(n).wait()
        h, p = divmod(n, parts)
        for k in range(deep // parts):
            lines = slice(k * BLK, (k + 1) * BLK)
            b_send[n, lines, :] = times_flag(b_send[n, lines, :], flags_b[h, slot * deep + p * (deep // parts) + k])
        done = [start + size for start, size in b_parts]
        if n + 1 == done[0]:
            pl.semaphore_wait(barrier, 2 + jnp.where(col == last_col, 1, 0) + jnp.where(col == relay, 1, 0))
        if n + 1 in done[:-1]:
            move_b(done.index(n + 1)).start()
        if n + 1 == done[0]:
            get_flags_a.start()
            get_own.start()
            for c in range(chunks):
                load_a(c).start()

    @pl.when(col != last_col)
    def _():
        move_b(last_part).start()

    @pl.when(col == last_col)
    def _():
        hand_over.start()

    get_own.wait()
    for h in range(halves):
        for k in range(deep):
            spot = (slice(k * BLK, (k + 1) * BLK), slice(h * BLK, (h + 1) * BLK))
            b_own[spot] = times_flag(b_own[spot], flags_b[h, k])
    get_flags_a.wait()

    def own_part(c, carry):
        load_a(c).wait()
        for g in range(group):
            lines = pl.ds(pl.multiple_of(c * span + g * BLK, BLK), BLK)
            for k in range(deep):
                block = a_tile[lines, k * BLK:(k + 1) * BLK]
                a_tile[lines, k * BLK:(k + 1) * BLK] = times_flag(block, flags_a[k, c * group + g])
        own_sum[lines_of(c), :] = jnp.dot(a_tile[lines_of(c), :], b_own[...], preferred_element_type=jnp.float32)
        return carry

    lax.fori_loop(0, chunks, own_part, 0)

    def send_out(first, last):
        for j in range(first, last):
            move_code(j).start()

    def next_part(h, c, carry):
        i = h * chunks + c
        tile = b_recv[h * parts:(h + 1) * parts].reshape(inner, BLK)
        value = jnp.dot(a_tile[lines_of(c), :], tile, preferred_element_type=jnp.float32)
        most = jnp.maximum(jnp.max(jnp.abs(value), axis=0, keepdims=True), TINY)
        step_send[i] = most * (1.0 / LEVELS)
        code_send[i] = jnp.round(value * (LEVELS / most)).astype(jnp.int32).astype(jnp.int16)
        return carry

    early = len(r_early)
    hold = (lax.rem(col, PLANE) == 0) | (col == relay)
    for h in range(halves):
        if h == halves - 1:

            @pl.when(jnp.logical_not(hold))
            def _():
                send_out(0, early)

            for j in range(len(b_parts)):
                move_b(j).wait_send()

            @pl.when(hold)
            def _():
                send_out(0, 1)

            @pl.when(col == relay)
            def _():
                hand_over.wait_recv()
                pass_along.start()

            @pl.when(hold)
            def _():
                send_out(1, early)

        for j, (start, _) in enumerate(b_parts):
            if start // parts == h:
                move_b(j).wait_recv()
        lax.fori_loop(0, chunks, functools.partial(next_part, h), 0)
        move_step(h).start()
    send_out(early, len(r_parts))

    for j, (start, size) in enumerate(r_parts):
        h = start // chunks

        def finish(c, carry, h=h):
            i = h * chunks + c
            code = code_recv[i].astype(jnp.int32).astype(jnp.float32)
            total = own_sum[lines_of(c), h * BLK:(h + 1) * BLK] + code * step_recv[i]
            out_tile[lines_of(c), h * BLK:(h + 1) * BLK] = total.astype(out_tile.dtype)
            return carry

        if start == h * chunks:
            move_step(h).wait_recv()
        move_code(j).wait_recv()
        lax.fori_loop(start - h * chunks, start - h * chunks + size, finish, 0)

    for h in range(halves):
        move_step(h).wait_send()
    for j in range(len(r_parts)):
        move_code(j).wait_send()

    @pl.when(col == relay)
    def _():
        pass_along.wait_send()


def pass_on(pieces, source, target, sem):
    span = source.shape[0] // pieces

    def put(n):
        return pltpu.make_async_copy(source.at[n * span:(n + 1) * span, :], target.at[n * span:(n + 1) * span, :], sem.at[n])

    for n in range(pieces):
        put(n).start()
    for n in range(pieces):
        put(n).wait()


def in_hbm(array):
    return pltpu.with_memory_space_constraint(array, pltpu.MemorySpace.HBM)


def body(mat_a, mat_b, mask_a, mask_b):
    rows, inner = mat_a.shape
    width = mat_b.shape[1]
    block_rows = mask_a.shape[0]
    group = next(g for g in (4, 2, 1) if block_rows % g == 0)
    parts = next(p for p in B_PARTS if inner // BLK % p == 0)
    span = group * BLK
    chunks = rows // span
    halves = width // BLK
    pieces, sends = halves * parts, halves * chunks
    b_copies, r_copies = len(b_runs(halves, parts)), sum(map(len, r_runs(halves, chunks)))
    dma = pltpu.SemaphoreType.DMA
    product = pl.pallas_call(
        functools.partial(kernel, group, parts),
        out_shape=pltpu.VMEM((rows, width), jnp.bfloat16),
        in_specs=[pl.BlockSpec(memory_space=pl.ANY)] * 4,
        out_specs=pl.BlockSpec(memory_space=pltpu.VMEM),
        scratch_shapes=[
            pltpu.SMEM(mask_a.shape[::-1], jnp.int32),
            pltpu.SMEM(mask_b.shape[::-1], jnp.int32),
            pltpu.VMEM((rows, inner), jnp.bfloat16),
            pltpu.VMEM((inner, width), jnp.bfloat16),
            pltpu.VMEM((pieces, inner // parts, BLK), jnp.bfloat16),
            pltpu.VMEM((pieces, inner // parts, BLK), jnp.bfloat16),
            pltpu.VMEM((rows, width), jnp.float32),
            pltpu.VMEM((sends, span, BLK), jnp.int16),
            pltpu.VMEM((sends, span, BLK), jnp.int16),
            pltpu.VMEM((sends, 1, BLK), jnp.float32),
            pltpu.VMEM((sends, 1, BLK), jnp.float32),
            pltpu.VMEM((1, inner // parts, BLK), jnp.bfloat16),
            dma((2,)), dma((chunks,)), dma((pieces + 1,)), dma((b_copies,)), dma((b_copies,)),
            dma((r_copies,)), dma((r_copies,)), dma((halves,)), dma((halves,)), dma((2,)),
        ],
        compiler_params=pltpu.CompilerParams(collective_id=0, has_side_effects=True, vmem_limit_bytes=52 * 1024 * 1024),
        name="cannon",
    )(mat_a, mat_b, in_hbm(mask_a.T), in_hbm(mask_b.T))
    return pl.pallas_call(
        functools.partial(pass_on, chunks),
        out_shape=jax.ShapeDtypeStruct(product.shape, product.dtype),
        in_specs=[pl.BlockSpec(memory_space=pl.ANY)],
        out_specs=pl.BlockSpec(memory_space=pl.ANY),
        scratch_shapes=[dma((chunks,))],
        compiler_params=pltpu.CompilerParams(vmem_limit_bytes=1024 * 1024),
        name="pass_on",
    )(product)


def solution(mesh):
    return jax.shard_map(
        body,
        mesh=mesh,
        in_specs=(P("row", "col"), P("row", "col"), P("row", "col"), P("row", "col")),
        out_specs=P("row", "col"),
        check_vma=False,
    )
```

```python
import functools

import jax
import jax.numpy as jnp
from jax import lax
from jax.experimental import pallas as pl
from jax.experimental.pallas import tpu as pltpu
from jax.sharding import PartitionSpec as P

BLK = 128
LEVELS = 32767.0
TINY = 1e-33
PLANE = 4
WAYS = 2
B_PARTS = (12, 6, 4, 3, 2, 1)
MESH = pl.DeviceIdType.MESH


def runs(start, sizes):
    found = []
    for size in sizes:
        if size > 0:
            found.append((start, size))
        start += size
    return found


def b_runs(halves, parts):
    found = []
    for h in range(halves - 1):
        found += runs(h * parts, (parts // 2, parts - parts // 2))
    return found + runs((halves - 1) * parts, (parts - WAYS,) + (1,) * WAYS)


def r_runs(halves, chunks):
    first = max(2 * chunks // 5, 1)
    found = []
    for h in range(halves - 1):
        found += runs(h * chunks, (first, chunks - first))
    return found, runs((halves - 1) * chunks, (chunks - 1, 1))


def times_flag(block, flag):
    scale = jnp.full(block.shape, flag.astype(jnp.float32)).astype(block.dtype)
    return block * scale


def kernel(
    group, parts,
    a_hbm, b_hbm, mask_a, mask_b, out_tile,
    flags_a, flags_b, a_tile, b_own, b_send, b_recv, own_sum, code_send, code_recv, step_send, step_recv, passing,
    f_sem, a_sem, b_sem, bs_sem, br_sem, cs_sem, cr_sem, ss_sem, sr_sem, p_sem,
):
    n_row, n_col = lax.axis_size("row"), lax.axis_size("col")
    row, col = lax.axis_index("row"), lax.axis_index("col")
    up, down = lax.rem(row + n_row - 1, n_row), lax.rem(row + 1, n_row)
    left, right = lax.rem(col + n_col - 1, n_col), lax.rem(col + 1, n_col)
    rows, inner = a_tile.shape
    width = b_own.shape[1]
    deep, halves = inner // BLK, width // BLK
    span = group * BLK
    chunks = rows // span
    cut = inner // parts
    pieces, sends = halves * parts, halves * chunks
    b_parts, (r_early, r_late) = b_runs(halves, parts), r_runs(halves, chunks)
    r_parts = r_early + r_late

    def lines_of(c):
        return pl.ds(pl.multiple_of(c * span, span), span)

    def load_a(c):
        return pltpu.make_async_copy(a_hbm.at[lines_of(c), :], a_tile.at[lines_of(c), :], a_sem.at[c])

    slot = jnp.where(row == 0, 1, 0)

    def load_send(n):
        h, p = divmod(n, parts)
        return pltpu.make_async_copy(
            b_hbm.at[pl.ds(pl.multiple_of(slot * inner + p * cut, cut), cut), h * BLK:(h + 1) * BLK], b_send.at[n], b_sem.at[n]
        )

    get_own = pltpu.make_async_copy(b_hbm.at[pl.ds(0, inner), :], b_own, b_sem.at[pieces])
    get_flags_b = pltpu.make_async_copy(mask_b, flags_b, f_sem.at[0])
    get_flags_a = pltpu.make_async_copy(mask_a, flags_a, f_sem.at[1])

    def move_b(j):
        start, size = b_parts[j]
        spot = slice(start, start + size)
        return pltpu.make_async_remote_copy(
            src_ref=b_send.at[spot], dst_ref=b_recv.at[spot], send_sem=bs_sem.at[j], recv_sem=br_sem.at[j],
            device_id={"row": up, "col": right}, device_id_type=MESH,
        )

    def move_code(j):
        start, size = r_parts[j]
        spot = slice(start, start + size)
        return pltpu.make_async_remote_copy(
            src_ref=code_send.at[spot], dst_ref=code_recv.at[spot], send_sem=cs_sem.at[j], recv_sem=cr_sem.at[j],
            device_id={"row": row, "col": left}, device_id_type=MESH,
        )

    def move_step(h):
        spot = slice(h * chunks, (h + 1) * chunks)
        return pltpu.make_async_remote_copy(
            src_ref=step_send.at[spot], dst_ref=step_recv.at[spot], send_sem=ss_sem.at[h], recv_sem=sr_sem.at[h],
            device_id={"row": row, "col": left}, device_id_type=MESH,
        )

    common = len(b_parts) - WAYS
    detours = ((n_col - 1, n_col - 2, (0, 1), None), (1, 2 * PLANE + 2, (0, 1), 0))

    def at_source(source, line):
        return col == source if line is None else (col == source) & (row == line)

    def beyond(column, line):
        return col == column if line is None else (col == column) & (row == (line + n_row - 1) % n_row)

    def first_leg(relay, w):
        start, size = b_parts[common + w]
        return pltpu.make_async_remote_copy(
            src_ref=b_send.at[start:start + size], dst_ref=passing.at[w:w + size],
            send_sem=bs_sem.at[common + w], recv_sem=p_sem.at[w],
            device_id={"row": up, "col": relay}, device_id_type=MESH,
        )

    def second_leg(source, w):
        start, size = b_parts[common + w]
        return pltpu.make_async_remote_copy(
            src_ref=passing.at[w:w + size], dst_ref=b_recv.at[start:start + size],
            send_sem=p_sem.at[WAYS + w], recv_sem=br_sem.at[common + w],
            device_id={"row": row, "col": (source + 1) % n_col}, device_id_type=MESH,
        )

    barrier = pltpu.get_barrier_semaphore()
    pl.semaphore_signal(barrier, inc=1, device_id={"row": down, "col": left}, device_id_type=MESH)
    pl.semaphore_signal(barrier, inc=1, device_id={"row": down, "col": col}, device_id_type=MESH)

    greets = 2
    for source, relay, _, line in detours:
        greets += jnp.where(at_source(source, line), 1, 0) + jnp.where(beyond(relay, line), 1, 0)

        @pl.when(beyond((source + 1) % n_col, line))
        def _(relay=relay):
            pl.semaphore_signal(barrier, inc=1, device_id={"row": row, "col": relay}, device_id_type=MESH)

        @pl.when(beyond(relay, line))
        def _(source=source):
            pl.semaphore_signal(barrier, inc=1, device_id={"row": down, "col": source}, device_id_type=MESH)

    get_flags_b.start()
    for n in range(pieces):
        load_send(n).start()
    get_flags_b.wait()
    for n in range(pieces):
        load_send(n).wait()
        h, p = divmod(n, parts)
        for k in range(deep // parts):
            lines = slice(k * BLK, (k + 1) * BLK)
            b_send[n, lines, :] = times_flag(b_send[n, lines, :], flags_b[h, slot * deep + p * (deep // parts) + k])
        done = [start + size for start, size in b_parts]
        if n + 1 == done[0]:
            pl.semaphore_wait(barrier, greets)
        if n + 1 in done[:common]:
            move_b(done.index(n + 1)).start()
        if n + 1 == done[0]:
            get_flags_a.start()
            get_own.start()
            for c in range(chunks):
                load_a(c).start()

    for w in range(WAYS):
        straight = True
        for source, relay, ways, line in detours:
            if w in ways:
                straight &= jnp.logical_not(at_source(source, line))

                @pl.when(at_source(source, line))
                def _(relay=relay, w=w):
                    first_leg(relay, w).start()

        @pl.when(straight)
        def _(w=w):
            move_b(common + w).start()

    get_own.wait()
    for h in range(halves):
        for k in range(deep):
            spot = (slice(k * BLK, (k + 1) * BLK), slice(h * BLK, (h + 1) * BLK))
            b_own[spot] = times_flag(b_own[spot], flags_b[h, k])
    get_flags_a.wait()

    def own_part(c, carry):
        load_a(c).wait()
        for g in range(group):
            lines = pl.ds(pl.multiple_of(c * span + g * BLK, BLK), BLK)
            for k in range(deep):
                block = a_tile[lines, k * BLK:(k + 1) * BLK]
                a_tile[lines, k * BLK:(k + 1) * BLK] = times_flag(block, flags_a[k, c * group + g])
        own_sum[lines_of(c), :] = jnp.dot(a_tile[lines_of(c), :], b_own[...], preferred_element_type=jnp.float32)
        return carry

    lax.fori_loop(0, chunks, own_part, 0)

    def send_out(first, last):
        for j in range(first, last):
            move_code(j).start()

    def next_part(h, c, carry):
        i = h * chunks + c
        tile = b_recv[h * parts:(h + 1) * parts].reshape(inner, BLK)
        value = jnp.dot(a_tile[lines_of(c), :], tile, preferred_element_type=jnp.float32)
        most = jnp.maximum(jnp.max(jnp.abs(value), axis=0, keepdims=True), TINY)
        step_send[i] = most * (1.0 / LEVELS)
        code_send[i] = jnp.round(value * (LEVELS / most)).astype(jnp.int32).astype(jnp.int16)
        return carry

    early = len(r_early)
    hold = lax.rem(col, PLANE) == 0
    for _, relay, _, line in detours:
        hold |= beyond(relay, line)
    for h in range(halves):
        if h == halves - 1:

            @pl.when(jnp.logical_not(hold))
            def _():
                send_out(0, early)

            for j in range(len(b_parts)):
                move_b(j).wait_send()

            @pl.when(hold)
            def _():
                send_out(0, 1)

            for source, relay, ways, line in detours:

                @pl.when(beyond(relay, line))
                def _(source=source, relay=relay, ways=ways):
                    for w in ways:
                        first_leg(relay, w).wait_recv()
                        second_leg(source, w).start()

            @pl.when(hold)
            def _():
                send_out(1, early)

        for j, (start, _) in enumerate(b_parts):
            if start // parts == h:
                move_b(j).wait_recv()
        lax.fori_loop(0, chunks, functools.partial(next_part, h), 0)
        move_step(h).start()
    send_out(early, len(r_parts))

    for j, (start, size) in enumerate(r_parts):
        h = start // chunks

        def finish(c, carry, h=h):
            i = h * chunks + c
            code = code_recv[i].astype(jnp.int32).astype(jnp.float32)
            total = own_sum[lines_of(c), h * BLK:(h + 1) * BLK] + code * step_recv[i]
            out_tile[lines_of(c), h * BLK:(h + 1) * BLK] = total.astype(out_tile.dtype)
            return carry

        if start == h * chunks:
            move_step(h).wait_recv()
        move_code(j).wait_recv()
        lax.fori_loop(start - h * chunks, start - h * chunks + size, finish, 0)

    for h in range(halves):
        move_step(h).wait_send()
    for j in range(len(r_parts)):
        move_code(j).wait_send()

    for source, relay, ways, line in detours:

        @pl.when(beyond(relay, line))
        def _(source=source, ways=ways):
            for w in ways:
                second_leg(source, w).wait_send()


def pass_on(pieces, source, target, sem):
    span = source.shape[0] // pieces

    def put(n):
        return pltpu.make_async_copy(source.at[n * span:(n + 1) * span, :], target.at[n * span:(n + 1) * span, :], sem.at[n])

    for n in range(pieces):
        put(n).start()
    for n in range(pieces):
        put(n).wait()


def in_hbm(array):
    return pltpu.with_memory_space_constraint(array, pltpu.MemorySpace.HBM)


def body(mat_a, mat_b, mask_a, mask_b):
    rows, inner = mat_a.shape
    width = mat_b.shape[1]
    block_rows = mask_a.shape[0]
    group = next(g for g in (4, 2, 1) if block_rows % g == 0)
    parts = next(p for p in B_PARTS if inner // BLK % p == 0)
    span = group * BLK
    chunks = rows // span
    halves = width // BLK
    pieces, sends = halves * parts, halves * chunks
    b_copies, r_copies = len(b_runs(halves, parts)), sum(map(len, r_runs(halves, chunks)))
    dma = pltpu.SemaphoreType.DMA
    product = pl.pallas_call(
        functools.partial(kernel, group, parts),
        out_shape=pltpu.VMEM((rows, width), jnp.bfloat16),
        in_specs=[pl.BlockSpec(memory_space=pl.ANY)] * 4,
        out_specs=pl.BlockSpec(memory_space=pltpu.VMEM),
        scratch_shapes=[
            pltpu.SMEM(mask_a.shape[::-1], jnp.int32),
            pltpu.SMEM(mask_b.shape[::-1], jnp.int32),
            pltpu.VMEM((rows, inner), jnp.bfloat16),
            pltpu.VMEM((inner, width), jnp.bfloat16),
            pltpu.VMEM((pieces, inner // parts, BLK), jnp.bfloat16),
            pltpu.VMEM((pieces, inner // parts, BLK), jnp.bfloat16),
            pltpu.VMEM((rows, width), jnp.float32),
            pltpu.VMEM((sends, span, BLK), jnp.int16),
            pltpu.VMEM((sends, span, BLK), jnp.int16),
            pltpu.VMEM((sends, 1, BLK), jnp.float32),
            pltpu.VMEM((sends, 1, BLK), jnp.float32),
            pltpu.VMEM((WAYS, inner // parts, BLK), jnp.bfloat16),
            dma((2,)), dma((chunks,)), dma((pieces + 1,)), dma((b_copies,)), dma((b_copies,)),
            dma((r_copies,)), dma((r_copies,)), dma((halves,)), dma((halves,)), dma((2 * WAYS,)),
        ],
        compiler_params=pltpu.CompilerParams(collective_id=0, has_side_effects=True, vmem_limit_bytes=52 * 1024 * 1024),
        name="cannon",
    )(mat_a, mat_b, in_hbm(mask_a.T), in_hbm(mask_b.T))
    return pl.pallas_call(
        functools.partial(pass_on, chunks),
        out_shape=jax.ShapeDtypeStruct(product.shape, product.dtype),
        in_specs=[pl.BlockSpec(memory_space=pl.ANY)],
        out_specs=pl.BlockSpec(memory_space=pl.ANY),
        scratch_shapes=[dma((chunks,))],
        compiler_params=pltpu.CompilerParams(vmem_limit_bytes=1024 * 1024),
        name="pass_on",
    )(product)


def solution(mesh):
    return jax.shard_map(
        body,
        mesh=mesh,
        in_specs=(P("row", "col"), P("row", "col"), P("row", "col"), P("row", "col")),
        out_specs=P("row", "col"),
        check_vma=False,
    )
```

```python
import functools

import jax
import jax.numpy as jnp
from jax import lax
from jax.experimental import pallas as pl
from jax.experimental.pallas import tpu as pltpu
from jax.sharding import PartitionSpec as P

BLK = 128
LEVELS = 32767.0
TINY = 1e-33
PLANE = 4
WAYS = 2
B_PARTS = (12, 6, 4, 3, 2, 1)
MESH = pl.DeviceIdType.MESH


def runs(start, sizes):
    found = []
    for size in sizes:
        if size > 0:
            found.append((start, size))
        start += size
    return found


def b_runs(halves, parts):
    found = []
    for h in range(halves - 1):
        found += runs(h * parts, (parts,))
    return found + runs((halves - 1) * parts, (parts - WAYS,) + (1,) * WAYS)


def r_runs(halves, chunks):
    first = max(2 * chunks // 5, 1)
    found = []
    for h in range(halves - 1):
        found += runs(h * chunks, (first, chunks - first))
    return found, runs((halves - 1) * chunks, (chunks - 1, 1))


def times_flag(block, flag):
    scale = jnp.full(block.shape, flag.astype(jnp.float32)).astype(block.dtype)
    return block * scale


def kernel(
    group, parts,
    a_hbm, b_hbm, mask_a, mask_b, out_tile,
    flags_a, flags_b, a_tile, b_own, b_send, b_recv, own_sum, code_send, code_recv, step_send, step_recv, passing,
    f_sem, a_sem, b_sem, bs_sem, br_sem, cs_sem, cr_sem, ss_sem, sr_sem, p_sem,
):
    n_row, n_col = lax.axis_size("row"), lax.axis_size("col")
    row, col = lax.axis_index("row"), lax.axis_index("col")
    up, down = lax.rem(row + n_row - 1, n_row), lax.rem(row + 1, n_row)
    left, right = lax.rem(col + n_col - 1, n_col), lax.rem(col + 1, n_col)
    rows, inner = a_tile.shape
    width = b_own.shape[1]
    deep, halves = inner // BLK, width // BLK
    span = group * BLK
    chunks = rows // span
    cut = inner // parts
    pieces, sends = halves * parts, halves * chunks
    b_parts, (r_early, r_late) = b_runs(halves, parts), r_runs(halves, chunks)
    r_parts = r_early + r_late

    def lines_of(c):
        return pl.ds(pl.multiple_of(c * span, span), span)

    def load_a(c):
        return pltpu.make_async_copy(a_hbm.at[lines_of(c), :], a_tile.at[lines_of(c), :], a_sem.at[c])

    slot = jnp.where(row == 0, 1, 0)

    def load_send(n):
        h, p = divmod(n, parts)
        return pltpu.make_async_copy(
            b_hbm.at[pl.ds(pl.multiple_of(slot * inner + p * cut, cut), cut), h * BLK:(h + 1) * BLK], b_send.at[n], b_sem.at[n]
        )

    get_own = pltpu.make_async_copy(b_hbm.at[pl.ds(0, inner), :], b_own, b_sem.at[pieces])
    get_flags_b = pltpu.make_async_copy(mask_b, flags_b, f_sem.at[0])
    get_flags_a = pltpu.make_async_copy(mask_a, flags_a, f_sem.at[1])

    def move_b(j):
        start, size = b_parts[j]
        spot = slice(start, start + size)
        return pltpu.make_async_remote_copy(
            src_ref=b_send.at[spot], dst_ref=b_recv.at[spot], send_sem=bs_sem.at[j], recv_sem=br_sem.at[j],
            device_id={"row": up, "col": right}, device_id_type=MESH,
        )

    def move_code(j):
        start, size = r_parts[j]
        spot = slice(start, start + size)
        return pltpu.make_async_remote_copy(
            src_ref=code_send.at[spot], dst_ref=code_recv.at[spot], send_sem=cs_sem.at[j], recv_sem=cr_sem.at[j],
            device_id={"row": row, "col": left}, device_id_type=MESH,
        )

    def move_step(h):
        spot = slice(h * chunks, (h + 1) * chunks)
        return pltpu.make_async_remote_copy(
            src_ref=step_send.at[spot], dst_ref=step_recv.at[spot], send_sem=ss_sem.at[h], recv_sem=sr_sem.at[h],
            device_id={"row": row, "col": left}, device_id_type=MESH,
        )

    common = len(b_parts) - WAYS
    detours = ((n_col - 1, n_col - 2, (0, 1), None), (1, 2 * PLANE + 2, (0, 1), 0))

    def at_source(source, line):
        return col == source if line is None else (col == source) & (row == line)

    def beyond(column, line):
        return col == column if line is None else (col == column) & (row == (line + n_row - 1) % n_row)

    def first_leg(relay, w):
        start, size = b_parts[common + w]
        return pltpu.make_async_remote_copy(
            src_ref=b_send.at[start:start + size], dst_ref=passing.at[w:w + size],
            send_sem=bs_sem.at[common + w], recv_sem=p_sem.at[w],
            device_id={"row": up, "col": relay}, device_id_type=MESH,
        )

    def second_leg(source, w):
        start, size = b_parts[common + w]
        return pltpu.make_async_remote_copy(
            src_ref=passing.at[w:w + size], dst_ref=b_recv.at[start:start + size],
            send_sem=p_sem.at[WAYS + w], recv_sem=br_sem.at[common + w],
            device_id={"row": row, "col": (source + 1) % n_col}, device_id_type=MESH,
        )

    barrier = pltpu.get_barrier_semaphore()
    pl.semaphore_signal(barrier, inc=1, device_id={"row": down, "col": left}, device_id_type=MESH)
    pl.semaphore_signal(barrier, inc=1, device_id={"row": down, "col": col}, device_id_type=MESH)

    greets = 2
    for source, relay, _, line in detours:
        greets += jnp.where(at_source(source, line), 1, 0) + jnp.where(beyond(relay, line), 1, 0)

        @pl.when(beyond((source + 1) % n_col, line))
        def _(relay=relay):
            pl.semaphore_signal(barrier, inc=1, device_id={"row": row, "col": relay}, device_id_type=MESH)

        @pl.when(beyond(relay, line))
        def _(source=source):
            pl.semaphore_signal(barrier, inc=1, device_id={"row": down, "col": source}, device_id_type=MESH)

    get_flags_b.start()
    for n in range(pieces):
        load_send(n).start()
    get_flags_b.wait()
    for n in range(pieces):
        load_send(n).wait()
        h, p = divmod(n, parts)
        for k in range(deep // parts):
            lines = slice(k * BLK, (k + 1) * BLK)
            b_send[n, lines, :] = times_flag(b_send[n, lines, :], flags_b[h, slot * deep + p * (deep // parts) + k])
        done = [start + size for start, size in b_parts]
        if n + 1 == done[0]:
            pl.semaphore_wait(barrier, greets)
        if n + 1 in done[:common]:
            move_b(done.index(n + 1)).start()
        if n + 1 == done[0]:
            get_flags_a.start()
            get_own.start()
            for c in range(chunks):
                load_a(c).start()

    for w in range(WAYS):
        straight = True
        for source, relay, ways, line in detours:
            if w in ways:
                straight &= jnp.logical_not(at_source(source, line))

                @pl.when(at_source(source, line))
                def _(relay=relay, w=w):
                    first_leg(relay, w).start()

        @pl.when(straight)
        def _(w=w):
            move_b(common + w).start()

    get_own.wait()
    for h in range(halves):
        for k in range(deep):
            spot = (slice(k * BLK, (k + 1) * BLK), slice(h * BLK, (h + 1) * BLK))
            b_own[spot] = times_flag(b_own[spot], flags_b[h, k])
    get_flags_a.wait()

    def own_part(c, carry):
        load_a(c).wait()
        for g in range(group):
            lines = pl.ds(pl.multiple_of(c * span + g * BLK, BLK), BLK)
            for k in range(deep):
                block = a_tile[lines, k * BLK:(k + 1) * BLK]
                a_tile[lines, k * BLK:(k + 1) * BLK] = times_flag(block, flags_a[k, c * group + g])
        own_sum[lines_of(c), :] = jnp.dot(a_tile[lines_of(c), :], b_own[...], preferred_element_type=jnp.float32)
        return carry

    lax.fori_loop(0, chunks, own_part, 0)

    def send_out(first, last):
        for j in range(first, last):
            move_code(j).start()

    def next_part(h, c, carry):
        i = h * chunks + c
        tile = b_recv[h * parts:(h + 1) * parts].reshape(inner, BLK)
        value = jnp.dot(a_tile[lines_of(c), :], tile, preferred_element_type=jnp.float32)
        most = jnp.maximum(jnp.max(jnp.abs(value), axis=0, keepdims=True), TINY)
        step_send[i] = most * (1.0 / LEVELS)
        code_send[i] = jnp.round(value * (LEVELS / most)).astype(jnp.int32).astype(jnp.int16)
        return carry

    early = len(r_early)
    hold = lax.rem(col, PLANE) == 0
    for _, relay, _, line in detours:
        hold |= beyond(relay, line)
    for h in range(halves):
        if h == halves - 1:

            @pl.when(jnp.logical_not(hold))
            def _():
                send_out(0, early)

            for j in range(len(b_parts)):
                move_b(j).wait_send()

            @pl.when(hold)
            def _():
                send_out(0, 1)

            for source, relay, ways, line in detours:

                @pl.when(beyond(relay, line))
                def _(source=source, relay=relay, ways=ways):
                    for w in ways:
                        first_leg(relay, w).wait_recv()
                        second_leg(source, w).start()

            @pl.when(hold)
            def _():
                send_out(1, early)

        for j, (start, _) in enumerate(b_parts):
            if start // parts == h:
                move_b(j).wait_recv()
        lax.fori_loop(0, chunks, functools.partial(next_part, h), 0)
        move_step(h).start()
    send_out(early, len(r_parts))

    for j, (start, size) in enumerate(r_parts):
        h = start // chunks

        def finish(c, carry, h=h):
            i = h * chunks + c
            code = code_recv[i].astype(jnp.int32).astype(jnp.float32)
            total = own_sum[lines_of(c), h * BLK:(h + 1) * BLK] + code * step_recv[i]
            out_tile[lines_of(c), h * BLK:(h + 1) * BLK] = total.astype(out_tile.dtype)
            return carry

        if start == h * chunks:
            move_step(h).wait_recv()
        move_code(j).wait_recv()
        lax.fori_loop(start - h * chunks, start - h * chunks + size, finish, 0)

    for h in range(halves):
        move_step(h).wait_send()
    for j in range(len(r_parts)):
        move_code(j).wait_send()

    for source, relay, ways, line in detours:

        @pl.when(beyond(relay, line))
        def _(source=source, ways=ways):
            for w in ways:
                second_leg(source, w).wait_send()


def pass_on(pieces, source, target, sem):
    span = source.shape[0] // pieces

    def put(n):
        return pltpu.make_async_copy(source.at[n * span:(n + 1) * span, :], target.at[n * span:(n + 1) * span, :], sem.at[n])

    for n in range(pieces):
        put(n).start()
    for n in range(pieces):
        put(n).wait()


def in_hbm(array):
    return pltpu.with_memory_space_constraint(array, pltpu.MemorySpace.HBM)


def body(mat_a, mat_b, mask_a, mask_b):
    rows, inner = mat_a.shape
    width = mat_b.shape[1]
    block_rows = mask_a.shape[0]
    group = next(g for g in (5, 4, 2, 1) if block_rows % g == 0)
    parts = next(p for p in B_PARTS if inner // BLK % p == 0)
    span = group * BLK
    chunks = rows // span
    halves = width // BLK
    pieces, sends = halves * parts, halves * chunks
    b_copies, r_copies = len(b_runs(halves, parts)), sum(map(len, r_runs(halves, chunks)))
    dma = pltpu.SemaphoreType.DMA
    product = pl.pallas_call(
        functools.partial(kernel, group, parts),
        out_shape=pltpu.VMEM((rows, width), jnp.bfloat16),
        in_specs=[pl.BlockSpec(memory_space=pl.ANY)] * 4,
        out_specs=pl.BlockSpec(memory_space=pltpu.VMEM),
        scratch_shapes=[
            pltpu.SMEM(mask_a.shape[::-1], jnp.int32),
            pltpu.SMEM(mask_b.shape[::-1], jnp.int32),
            pltpu.VMEM((rows, inner), jnp.bfloat16),
            pltpu.VMEM((inner, width), jnp.bfloat16),
            pltpu.VMEM((pieces, inner // parts, BLK), jnp.bfloat16),
            pltpu.VMEM((pieces, inner // parts, BLK), jnp.bfloat16),
            pltpu.VMEM((rows, width), jnp.float32),
            pltpu.VMEM((sends, span, BLK), jnp.int16),
            pltpu.VMEM((sends, span, BLK), jnp.int16),
            pltpu.VMEM((sends, 1, BLK), jnp.float32),
            pltpu.VMEM((sends, 1, BLK), jnp.float32),
            pltpu.VMEM((WAYS, inner // parts, BLK), jnp.bfloat16),
            dma((2,)), dma((chunks,)), dma((pieces + 1,)), dma((b_copies,)), dma((b_copies,)),
            dma((r_copies,)), dma((r_copies,)), dma((halves,)), dma((halves,)), dma((2 * WAYS,)),
        ],
        compiler_params=pltpu.CompilerParams(collective_id=0, has_side_effects=True, vmem_limit_bytes=52 * 1024 * 1024),
        name="cannon",
    )(mat_a, mat_b, in_hbm(mask_a.T), in_hbm(mask_b.T))
    return pl.pallas_call(
        functools.partial(pass_on, chunks),
        out_shape=jax.ShapeDtypeStruct(product.shape, product.dtype),
        in_specs=[pl.BlockSpec(memory_space=pl.ANY)],
        out_specs=pl.BlockSpec(memory_space=pl.ANY),
        scratch_shapes=[dma((chunks,))],
        compiler_params=pltpu.CompilerParams(vmem_limit_bytes=1024 * 1024),
        name="pass_on",
    )(product)


def solution(mesh):
    return jax.shard_map(
        body,
        mesh=mesh,
        in_specs=(P("row", "col"), P("row", "col"), P("row", "col"), P("row", "col")),
        out_specs=P("row", "col"),
        check_vma=False,
    )
```

```python
import functools

import jax
import jax.numpy as jnp
from jax import lax
from jax.experimental import pallas as pl
from jax.experimental.pallas import tpu as pltpu
from jax.sharding import PartitionSpec as P

BLK = 128
LEVELS = 32767.0
TINY = 1e-33
PLANE = 4
WAYS = 3
B_PARTS = (12, 6, 4, 3, 2, 1)
MESH = pl.DeviceIdType.MESH


def runs(start, sizes):
    found = []
    for size in sizes:
        if size > 0:
            found.append((start, size))
        start += size
    return found


def b_runs(halves, parts):
    found = []
    for h in range(halves - 1):
        found += runs(h * parts, (parts // 2, parts - parts // 2))
    return found + runs((halves - 1) * parts, (parts - WAYS,) + (1,) * WAYS)


def r_runs(halves, chunks):
    first = max(2 * chunks // 5, 1)
    found = []
    for h in range(halves - 1):
        found += runs(h * chunks, (first, chunks - first))
    return found, runs((halves - 1) * chunks, (chunks - 1, 1))


def times_flag(block, flag):
    scale = jnp.full(block.shape, flag.astype(jnp.float32)).astype(block.dtype)
    return block * scale


def kernel(
    group, parts,
    a_hbm, b_hbm, mask_a, mask_b, out_tile,
    flags_a, flags_b, a_tile, b_own, b_send, b_recv, own_sum, code_send, code_recv, step_send, step_recv, passing,
    f_sem, a_sem, b_sem, bs_sem, br_sem, cs_sem, cr_sem, ss_sem, sr_sem, p_sem,
):
    n_row, n_col = lax.axis_size("row"), lax.axis_size("col")
    row, col = lax.axis_index("row"), lax.axis_index("col")
    up, down = lax.rem(row + n_row - 1, n_row), lax.rem(row + 1, n_row)
    left, right = lax.rem(col + n_col - 1, n_col), lax.rem(col + 1, n_col)
    rows, inner = a_tile.shape
    width = b_own.shape[1]
    deep, halves = inner // BLK, width // BLK
    span = group * BLK
    chunks = rows // span
    cut = inner // parts
    pieces, sends = halves * parts, halves * chunks
    b_parts, (r_early, r_late) = b_runs(halves, parts), r_runs(halves, chunks)
    r_parts = r_early + r_late

    def lines_of(c):
        return pl.ds(pl.multiple_of(c * span, span), span)

    def load_a(c):
        return pltpu.make_async_copy(a_hbm.at[lines_of(c), :], a_tile.at[lines_of(c), :], a_sem.at[c])

    slot = jnp.where(row == 0, 1, 0)

    def load_send(n):
        h, p = divmod(n, parts)
        return pltpu.make_async_copy(
            b_hbm.at[pl.ds(pl.multiple_of(slot * inner + p * cut, cut), cut), h * BLK:(h + 1) * BLK], b_send.at[n], b_sem.at[n]
        )

    get_own = pltpu.make_async_copy(b_hbm.at[pl.ds(0, inner), :], b_own, b_sem.at[pieces])
    get_flags_b = pltpu.make_async_copy(mask_b, flags_b, f_sem.at[0])
    get_flags_a = pltpu.make_async_copy(mask_a, flags_a, f_sem.at[1])

    def move_b(j):
        start, size = b_parts[j]
        spot = slice(start, start + size)
        return pltpu.make_async_remote_copy(
            src_ref=b_send.at[spot], dst_ref=b_recv.at[spot], send_sem=bs_sem.at[j], recv_sem=br_sem.at[j],
            device_id={"row": up, "col": right}, device_id_type=MESH,
        )

    def move_code(j):
        start, size = r_parts[j]
        spot = slice(start, start + size)
        return pltpu.make_async_remote_copy(
            src_ref=code_send.at[spot], dst_ref=code_recv.at[spot], send_sem=cs_sem.at[j], recv_sem=cr_sem.at[j],
            device_id={"row": row, "col": left}, device_id_type=MESH,
        )

    def move_step(h):
        spot = slice(h * chunks, (h + 1) * chunks)
        return pltpu.make_async_remote_copy(
            src_ref=step_send.at[spot], dst_ref=step_recv.at[spot], send_sem=ss_sem.at[h], recv_sem=sr_sem.at[h],
            device_id={"row": row, "col": left}, device_id_type=MESH,
        )

    common = len(b_parts) - WAYS
    detours = ((n_col - 1, n_col - 2, (0, 1, 2), 1), (n_col - 1, PLANE + 2, (1, 2), 0), (1, 2 * PLANE + 2, (1, 2), 1))

    def at_source(source, line):
        return col == source if line is None else (col == source) & (row == line)

    def beyond(column, line):
        return col == column if line is None else (col == column) & (row == (line + n_row - 1) % n_row)

    def first_leg(relay, w):
        start, size = b_parts[common + w]
        return pltpu.make_async_remote_copy(
            src_ref=b_send.at[start:start + size], dst_ref=passing.at[w:w + size],
            send_sem=bs_sem.at[common + w], recv_sem=p_sem.at[w],
            device_id={"row": up, "col": relay}, device_id_type=MESH,
        )

    def second_leg(source, w):
        start, size = b_parts[common + w]
        return pltpu.make_async_remote_copy(
            src_ref=passing.at[w:w + size], dst_ref=b_recv.at[start:start + size],
            send_sem=p_sem.at[WAYS + w], recv_sem=br_sem.at[common + w],
            device_id={"row": row, "col": (source + 1) % n_col}, device_id_type=MESH,
        )

    barrier = pltpu.get_barrier_semaphore()
    pl.semaphore_signal(barrier, inc=1, device_id={"row": down, "col": left}, device_id_type=MESH)
    pl.semaphore_signal(barrier, inc=1, device_id={"row": down, "col": col}, device_id_type=MESH)

    greets = 2
    for source, relay, _, line in detours:
        greets += jnp.where(at_source(source, line), 1, 0) + jnp.where(beyond(relay, line), 1, 0)

        @pl.when(beyond((source + 1) % n_col, line))
        def _(relay=relay):
            pl.semaphore_signal(barrier, inc=1, device_id={"row": row, "col": relay}, device_id_type=MESH)

        @pl.when(beyond(relay, line))
        def _(source=source):
            pl.semaphore_signal(barrier, inc=1, device_id={"row": down, "col": source}, device_id_type=MESH)

    get_flags_b.start()
    for n in range(pieces):
        load_send(n).start()
    get_flags_b.wait()
    for n in range(pieces):
        load_send(n).wait()
        h, p = divmod(n, parts)
        for k in range(deep // parts):
            lines = slice(k * BLK, (k + 1) * BLK)
            b_send[n, lines, :] = times_flag(b_send[n, lines, :], flags_b[h, slot * deep + p * (deep // parts) + k])
        done = [start + size for start, size in b_parts]
        if n + 1 == done[0]:
            pl.semaphore_wait(barrier, greets)
        if n + 1 in done[:common]:
            move_b(done.index(n + 1)).start()
        if n + 1 == done[0]:
            get_flags_a.start()
            get_own.start()
            for c in range(chunks):
                load_a(c).start()

    for w in range(WAYS):
        straight = True
        for source, relay, ways, line in detours:
            if w in ways:
                straight &= jnp.logical_not(at_source(source, line))

                @pl.when(at_source(source, line))
                def _(relay=relay, w=w):
                    first_leg(relay, w).start()

        @pl.when(straight)
        def _(w=w):
            move_b(common + w).start()

    get_own.wait()
    for h in range(halves):
        for k in range(deep):
            spot = (slice(k * BLK, (k + 1) * BLK), slice(h * BLK, (h + 1) * BLK))
            b_own[spot] = times_flag(b_own[spot], flags_b[h, k])
    get_flags_a.wait()

    def own_part(c, carry):
        load_a(c).wait()
        for g in range(group):
            lines = pl.ds(pl.multiple_of(c * span + g * BLK, BLK), BLK)
            for k in range(deep):
                block = a_tile[lines, k * BLK:(k + 1) * BLK]
                a_tile[lines, k * BLK:(k + 1) * BLK] = times_flag(block, flags_a[k, c * group + g])
        own_sum[lines_of(c), :] = jnp.dot(a_tile[lines_of(c), :], b_own[...], preferred_element_type=jnp.float32)
        return carry

    lax.fori_loop(0, chunks, own_part, 0)

    def send_out(first, last):
        for j in range(first, last):
            move_code(j).start()

    def next_part(h, c, carry):
        i = h * chunks + c
        tile = b_recv[h * parts:(h + 1) * parts].reshape(inner, BLK)
        value = jnp.dot(a_tile[lines_of(c), :], tile, preferred_element_type=jnp.float32)
        most = jnp.maximum(jnp.max(jnp.abs(value), axis=0, keepdims=True), TINY)
        step_send[i] = most * (1.0 / LEVELS)
        code_send[i] = jnp.round(value * (LEVELS / most)).astype(jnp.int32).astype(jnp.int16)
        return carry

    early = len(r_early)
    hold = lax.rem(col, PLANE) == 0
    for _, relay, _, line in detours:
        hold |= beyond(relay, line)
    for h in range(halves):
        if h == halves - 1:

            @pl.when(jnp.logical_not(hold))
            def _():
                send_out(0, early)

            for j in range(len(b_parts)):
                move_b(j).wait_send()

            @pl.when(hold)
            def _():
                send_out(0, 1)

            for source, relay, ways, line in detours:

                @pl.when(beyond(relay, line))
                def _(source=source, relay=relay, ways=ways):
                    for w in ways:
                        first_leg(relay, w).wait_recv()
                        second_leg(source, w).start()

            @pl.when(hold)
            def _():
                send_out(1, early)

        for j, (start, _) in enumerate(b_parts):
            if start // parts == h:
                move_b(j).wait_recv()
        lax.fori_loop(0, chunks, functools.partial(next_part, h), 0)
        move_step(h).start()
    send_out(early, len(r_parts))

    for j, (start, size) in enumerate(r_parts):
        h = start // chunks

        def finish(c, carry, h=h):
            i = h * chunks + c
            code = code_recv[i].astype(jnp.int32).astype(jnp.float32)
            total = own_sum[lines_of(c), h * BLK:(h + 1) * BLK] + code * step_recv[i]
            out_tile[lines_of(c), h * BLK:(h + 1) * BLK] = total.astype(out_tile.dtype)
            return carry

        if start == h * chunks:
            move_step(h).wait_recv()
        move_code(j).wait_recv()
        lax.fori_loop(start - h * chunks, start - h * chunks + size, finish, 0)

    for h in range(halves):
        move_step(h).wait_send()
    for j in range(len(r_parts)):
        move_code(j).wait_send()

    for source, relay, ways, line in detours:

        @pl.when(beyond(relay, line))
        def _(source=source, ways=ways):
            for w in ways:
                second_leg(source, w).wait_send()


def pass_on(pieces, source, target, sem):
    span = source.shape[0] // pieces

    def put(n):
        return pltpu.make_async_copy(source.at[n * span:(n + 1) * span, :], target.at[n * span:(n + 1) * span, :], sem.at[n])

    for n in range(pieces):
        put(n).start()
    for n in range(pieces):
        put(n).wait()


def in_hbm(array):
    return pltpu.with_memory_space_constraint(array, pltpu.MemorySpace.HBM)


def body(mat_a, mat_b, mask_a, mask_b):
    rows, inner = mat_a.shape
    width = mat_b.shape[1]
    block_rows = mask_a.shape[0]
    group = next(g for g in (4, 2, 1) if block_rows % g == 0)
    parts = next(p for p in B_PARTS if inner // BLK % p == 0)
    span = group * BLK
    chunks = rows // span
    halves = width // BLK
    pieces, sends = halves * parts, halves * chunks
    b_copies, r_copies = len(b_runs(halves, parts)), sum(map(len, r_runs(halves, chunks)))
    dma = pltpu.SemaphoreType.DMA
    product = pl.pallas_call(
        functools.partial(kernel, group, parts),
        out_shape=pltpu.VMEM((rows, width), jnp.bfloat16),
        in_specs=[pl.BlockSpec(memory_space=pl.ANY)] * 4,
        out_specs=pl.BlockSpec(memory_space=pltpu.VMEM),
        scratch_shapes=[
            pltpu.SMEM(mask_a.shape[::-1], jnp.int32),
            pltpu.SMEM(mask_b.shape[::-1], jnp.int32),
            pltpu.VMEM((rows, inner), jnp.bfloat16),
            pltpu.VMEM((inner, width), jnp.bfloat16),
            pltpu.VMEM((pieces, inner // parts, BLK), jnp.bfloat16),
            pltpu.VMEM((pieces, inner // parts, BLK), jnp.bfloat16),
            pltpu.VMEM((rows, width), jnp.float32),
            pltpu.VMEM((sends, span, BLK), jnp.int16),
            pltpu.VMEM((sends, span, BLK), jnp.int16),
            pltpu.VMEM((sends, 1, BLK), jnp.float32),
            pltpu.VMEM((sends, 1, BLK), jnp.float32),
            pltpu.VMEM((WAYS, inner // parts, BLK), jnp.bfloat16),
            dma((2,)), dma((chunks,)), dma((pieces + 1,)), dma((b_copies,)), dma((b_copies,)),
            dma((r_copies,)), dma((r_copies,)), dma((halves,)), dma((halves,)), dma((2 * WAYS,)),
        ],
        compiler_params=pltpu.CompilerParams(collective_id=0, has_side_effects=True, vmem_limit_bytes=52 * 1024 * 1024),
        name="cannon",
    )(mat_a, mat_b, in_hbm(mask_a.T), in_hbm(mask_b.T))
    return pl.pallas_call(
        functools.partial(pass_on, chunks),
        out_shape=jax.ShapeDtypeStruct(product.shape, product.dtype),
        in_specs=[pl.BlockSpec(memory_space=pl.ANY)],
        out_specs=pl.BlockSpec(memory_space=pl.ANY),
        scratch_shapes=[dma((chunks,))],
        compiler_params=pltpu.CompilerParams(vmem_limit_bytes=1024 * 1024),
        name="pass_on",
    )(product)


def solution(mesh):
    return jax.shard_map(
        body,
        mesh=mesh,
        in_specs=(P("row", "col"), P("row", "col"), P("row", "col"), P("row", "col")),
        out_specs=P("row", "col"),
        check_vma=False,
    )
```
